1024 devices in a mesh: tok: 128 (over y, z), head: 8 (over x, core).
Axes of the slice: x: 4, y: 4, z: 32, core: 2. Of those that a mesh axis runs over, the one named last changes fastest.
Arguments:
- query: bfloat16 [16384, 8192], P('tok', 'head'), may hold values from -5 to 5
- keys: bfloat16 [16384, 1024], P(('tok', 'head')), may hold values from -5 to 5
- values: bfloat16 [16384, 1024], P(('tok', 'head')), may hold values from -6 to 6
- out_grad: bfloat16 [16384, 8192], P('tok', 'head'), may hold values from -6 to 6
- log_norm: float32 [64, 16384], P('head', 'tok'), may hold values from 4 to 6
- row_dot: float32 [64, 16384], P('head', 'tok'), may hold values from -24 to 24
- doc_start: int32 [16384], replicated, may hold values from 0 to 16383, as said below
- spans: int32 [128], replicated, may hold values from 1 to 6, as said below
Outputs:
- query_grad: bfloat16 [16384, 8192], P('tok', 'head')
- key_grad: bfloat16 [16384, 1024], P('tok', 'head')
- value_grad: bfloat16 [16384, 1024], P('tok', 'head')
The draws below stay inside these ranges and needn't reach their ends.
Inputs may be any that keep to these rules, and one draw needn't show every extreme that they name: doc_start[t] <= t, doc_start[0] = 0, doc_start never falls along t, and doc_start[t] = t where a document begins; the last position always begins a document of one token. Query block g (tokens g * 128 to g * 128 + 127) reads the spans[g] key blocks that end with block g itself. In every draw at least one query block has span 6.
All inputs are finite; a program needn't handle non-finite values.
Results may differ from the reference program's by a relative error of at most 0.008.
Values may be sent and summed in bfloat16 or wider, within the bound.
A program may use at most 32 MiB of HBM per device.

```python
import math
import jax
import jax.numpy as jnp
from jax import lax

HEADS = 64
KV_HEADS = 8
HEAD_DIM = 128
QBLOCK = 128
SPAN_MAX = 6
QB_DEV = 1
TOKENS = 16384
QBLOCKS = 128


def scaled_rows(key, rows, columns):
    return jnp.clip(jax.random.normal(key, (rows, columns), jnp.float32), -5.0, 5.0)


def draw_query(key, part):
    return scaled_rows(jax.random.fold_in(key, 11), TOKENS, HEADS * HEAD_DIM).astype(jnp.bfloat16)


def draw_keys(key, part):
    return scaled_rows(jax.random.fold_in(key, 23), TOKENS, KV_HEADS * HEAD_DIM).astype(jnp.bfloat16)


def draw_doc_start(key, part):
    positions = jnp.arange(TOKENS, dtype=jnp.int32)
    marks = jax.random.randint(jax.random.fold_in(key, 31), (TOKENS,), 0, 8 * QBLOCK) == 0
    marks = marks | (positions == TOKENS - 1)
    begins = jnp.where(marks, positions, 0).astype(jnp.int32)
    return lax.cummax(begins, axis=0).astype(jnp.int32)


def draw_spans(key, part):
    groups = QBLOCKS // QB_DEV
    base_key = jax.random.fold_in(key, 47)
    first_key, second_key, third_key = jax.random.split(base_key, 3)
    heavy = jax.random.randint(first_key, (groups,), 0, 16) == 0
    chosen = jax.random.randint(third_key, (), 0, groups)
    heavy = heavy | (jnp.arange(groups, dtype=jnp.int32) == chosen)
    light = jax.random.randint(second_key, (groups, QB_DEV), 1, 4)
    spread = jnp.where(heavy[:, None], SPAN_MAX, light)
    return spread.reshape(QBLOCKS).astype(jnp.int32)


def shard_levels(stream_key, extent, cuts, least, high):
    def one(position, blocks):
        heights = jax.random.uniform(jax.random.fold_in(jax.random.fold_in(stream_key, 6), position), (blocks,), jnp.float32, least / len(cuts), high / len(cuts))
        return jnp.repeat(jnp.exp(heights), extent[position] // blocks).reshape((-1,) + (1,) * (len(extent) - position - 1))

    factor_of = one(*cuts[0])
    for cut in cuts[1:]:
        factor_of = factor_of * one(*cut)
    return factor_of


def gaussian(rng, shape, scale, reach, cuts=(), held_as=jnp.bfloat16):
    array = jax.random.normal(rng, shape, jnp.float32) * scale
    if len(cuts) > 0:
        array = shard_levels(rng, shape, cuts, -0.22, 0.18) * array
    return jnp.clip(array, min=-reach, max=reach).astype(held_as)


def setup_inputs(seed: int = 0) -> dict:
    seeds = jax.random.split(jax.random.key(seed), 9)
    return {
        "query": draw_query(jax.random.fold_in(seeds[8], 71), 0),
        "keys": draw_keys(jax.random.fold_in(seeds[8], 71), 0),
        "values": gaussian(seeds[2], (TOKENS, KV_HEADS * HEAD_DIM), 1.0, 6.0, ((0, 1024),)),
        "out_grad": gaussian(seeds[3], (TOKENS, HEADS * HEAD_DIM), 1.0, 6.0, ((0, 128), (1, 8))),
        "log_norm": jnp.clip(4.0 + 2.0 * jax.random.uniform(seeds[4], (HEADS, TOKENS), jnp.float32) ** shard_levels(seeds[4], (HEADS, TOKENS), ((0, 8), (1, 128)), -0.2, 0.2), 4.0, 6.0),
        "row_dot": gaussian(seeds[5], (HEADS, TOKENS), 4.0, 24.0, ((0, 8), (1, 128)), jnp.float32),
        "doc_start": draw_doc_start(jax.random.fold_in(seeds[8], 71), 0),
        "spans": draw_spans(jax.random.fold_in(seeds[8], 71), 0),
    }


def reference(query, keys, values, out_grad, log_norm, row_dot, doc_start, spans):
    group_size = HEADS // KV_HEADS
    head_scale = 1.0 / math.sqrt(HEAD_DIM)
    pad_rows = (SPAN_MAX - 1) * QBLOCK
    window_rows = SPAN_MAX * QBLOCK
    filler = jnp.zeros((pad_rows, KV_HEADS * HEAD_DIM), keys.dtype)
    key_wide = jnp.concatenate([filler, keys], axis=0).reshape(-1, KV_HEADS, HEAD_DIM)
    value_wide = jnp.concatenate([filler, values], axis=0).reshape(-1, KV_HEADS, HEAD_DIM)
    query_blocks = query.reshape(QBLOCKS, QBLOCK, KV_HEADS, group_size, HEAD_DIM)
    outgrad_blocks = out_grad.reshape(QBLOCKS, QBLOCK, KV_HEADS, group_size, HEAD_DIM)
    norm_blocks = log_norm.reshape(KV_HEADS, group_size, QBLOCKS, QBLOCK).transpose(2, 0, 1, 3)
    dot_blocks = row_dot.reshape(KV_HEADS, group_size, QBLOCKS, QBLOCK).transpose(2, 0, 1, 3)
    start_blocks = doc_start.reshape(QBLOCKS, QBLOCK)
    row_index = jnp.arange(QBLOCK, dtype=jnp.int32)
    window_index = jnp.arange(window_rows, dtype=jnp.int32)

    def one_block(totals, inputs):
        key_total, value_total = totals
        block_index, query_block, outgrad_block, norm_block, dot_block, start_block, span_count = inputs
        anchor = (block_index * QBLOCK).astype(jnp.int32)
        key_window = lax.dynamic_slice_in_dim(key_wide, anchor, window_rows, 0).astype(jnp.float32)
        value_window = lax.dynamic_slice_in_dim(value_wide, anchor, window_rows, 0).astype(jnp.float32)
        query_pos = anchor + row_index
        key_pos = anchor - pad_rows + window_index
        key_blockid = block_index - (SPAN_MAX - 1) + window_index // QBLOCK
        allowed = (key_pos[None, :] <= query_pos[:, None]) & (key_pos[None, :] >= start_block[:, None])
        allowed = allowed & (key_blockid[None, :] > block_index - span_count)
        query_wide = query_block.astype(jnp.float32)
        outgrad_wide = outgrad_block.astype(jnp.float32)
        scores = jnp.einsum('qagd,kad->agqk', query_wide, key_window) * head_scale
        probs = jnp.where(allowed[None, None], jnp.exp(scores - norm_block[..., None]), 0.0)
        probs_low = lax.optimization_barrier(probs.astype(jnp.bfloat16)).astype(jnp.float32)
        value_term = jnp.einsum('agqk,qagd->kad', probs_low, outgrad_wide)
        prob_grad = jnp.einsum('qagd,kad->agqk', outgrad_wide, value_window)
        score_grad = (probs * (prob_grad - dot_block[..., None])).astype(jnp.bfloat16)
        score_grad = lax.optimization_barrier(score_grad).astype(jnp.float32)
        query_term = jnp.einsum('agqk,kad->qagd', score_grad, key_window) * head_scale
        key_term = jnp.einsum('agqk,qagd->kad', score_grad, query_wide) * head_scale
        key_old = lax.dynamic_slice_in_dim(key_total, anchor, window_rows, 0)
        key_total = lax.dynamic_update_slice_in_dim(key_total, key_old + key_term, anchor, 0)
        value_old = lax.dynamic_slice_in_dim(value_total, anchor, window_rows, 0)
        value_total = lax.dynamic_update_slice_in_dim(value_total, value_old + value_term, anchor, 0)
        return ((key_total, value_total), query_term)
    zero_total = jnp.zeros((pad_rows + TOKENS, KV_HEADS, HEAD_DIM), jnp.float32)
    block_ids = jnp.arange(QBLOCKS, dtype=jnp.int32)
    finals, query_terms = lax.scan(one_block, (zero_total, zero_total), (block_ids, query_blocks, outgrad_blocks, norm_blocks, dot_blocks, start_blocks, spans))
    key_total, value_total = finals
    query_grad = query_terms.reshape(TOKENS, HEADS * HEAD_DIM).astype(jnp.bfloat16)
    key_grad = key_total[pad_rows:].reshape(TOKENS, KV_HEADS * HEAD_DIM).astype(jnp.bfloat16)
    value_grad = value_total[pad_rows:].reshape(TOKENS, KV_HEADS * HEAD_DIM).astype(jnp.bfloat16)
    return (query_grad, key_grad, value_grad)
```

```python
import functools
import math

import jax
import jax.numpy as jnp
from jax import lax
from jax.experimental import pallas as pl
from jax.experimental.pallas import tpu as pltpu
from jax.sharding import PartitionSpec as P

HEADS = 64
KV_HEADS = 8
HEAD_DIM = 128
QBLOCK = 128
REACH = 5
GROUP = HEADS // KV_HEADS
PIECES = 2
MESH = pl.DeviceIdType.MESH
FAR = 1 << 30

NT = (((1,), (1,)), ((), ()))
NN = (((1,), (0,)), ((), ()))


def matmul(a, b, dims):
    return lax.dot_general(a, b, dims, preferred_element_type=jnp.float32)


def kernel(
    n_tok,
    n_head,
    query_hbm,
    keys_hbm,
    values_hbm,
    outgrad_hbm,
    norm_hbm,
    dot_hbm,
    starts_hbm,
    spans_hbm,
    dq_hbm,
    dk_hbm,
    dv_hbm,
    q_s,
    do_s,
    norm_s,
    dot_s,
    starts_s,
    spans_s,
    key_win,
    value_win,
    key_t,
    ds_all,
    send_buf,
    recv_buf,
    own_buf,
    far_buf,
    dq_s,
    out_s,
    in_sem,
    a2a_send,
    own_sem,
    kv_send,
    kv_recv,
    grad_send,
    grad_recv,
    out_sem,
):
    scale = 1.0 / math.sqrt(HEAD_DIM)
    tok = lax.axis_index("tok")
    head = lax.axis_index("head")
    rows = QBLOCK // n_head
    half = QBLOCK // PIECES

    def tok_at(step):
        return lax.rem(tok + (step + n_tok), n_tok)

    slot_rows = pl.ds(pl.multiple_of(head * rows, rows), rows)
    my_half = lax.div(head, n_head // PIECES)

    def columns(h):
        return pl.ds(pl.multiple_of(h * HEAD_DIM, HEAD_DIM), HEAD_DIM)

    own_copies = []
    for side, (source, window) in enumerate(((keys_hbm, key_win), (values_hbm, value_win))):
        own_copies.append(
            pltpu.make_async_copy(
                source.at[:, columns(head)], window.at[0, slot_rows, :], own_sem.at[side, my_half]
            )
        )
    for copy in own_copies:
        copy.start()
    loads = []
    for h in range(GROUP):
        block = pl.ds(h * QBLOCK, QBLOCK)
        cols = pl.ds(h * HEAD_DIM, HEAD_DIM)
        loads.append(pltpu.make_async_copy(query_hbm.at[:, cols], q_s.at[block, :], in_sem.at[h]))
        loads.append(
            pltpu.make_async_copy(outgrad_hbm.at[:, cols], do_s.at[block, :], in_sem.at[GROUP + h])
        )
    base = 2 * GROUP
    loads.append(pltpu.make_async_copy(norm_hbm, norm_s, in_sem.at[base]))
    loads.append(pltpu.make_async_copy(dot_hbm, dot_s, in_sem.at[base + 1]))
    loads.append(pltpu.make_async_copy(starts_hbm, starts_s, in_sem.at[base + 2]))
    loads.append(pltpu.make_async_copy(spans_hbm, spans_s, in_sem.at[base + 3]))
    for copy in loads:
        copy.start()

    barrier = pltpu.get_barrier_semaphore()
    for step in range(1, n_head):
        pl.semaphore_signal(
            barrier, 1, device_id={"head": lax.rem(head + step, n_head)}, device_id_type=MESH
        )
    for step in (1, -1):
        pl.semaphore_signal(barrier, 1, device_id={"tok": tok_at(step)}, device_id_type=MESH)
    pl.semaphore_wait(barrier, n_head + 1)

    spreads = []
    for side, (source, window) in enumerate(((keys_hbm, key_win), (values_hbm, value_win))):
        for step in range(1, n_head):
            peer = lax.rem(head + step, n_head)
            copy = pltpu.make_async_remote_copy(
                src_ref=source.at[:, columns(peer)],
                dst_ref=window.at[0, slot_rows, :],
                send_sem=a2a_send.at[side, step - 1],
                recv_sem=own_sem.at[side, my_half],
                device_id={"head": peer},
                device_id_type=MESH,
            )
            copy.start()
            spreads.append(copy)

    def piece(slot, side, part):
        window = (key_win, value_win)[side]
        return window.at[slot, pl.ds(part * half, half), :]

    forwards = []

    def forward(slot, side, part):
        copy = pltpu.make_async_remote_copy(
            src_ref=piece(slot, side, part),
            dst_ref=piece(slot + 1, side, part),
            send_sem=kv_send.at[slot, side, part],
            recv_sem=kv_recv.at[slot, side, part],
            device_id={"tok": tok_at(1)},
            device_id_type=MESH,
        )
        copy.start()
        forwards.append(copy)
        return copy

    for side in range(2):
        for part in range(PIECES):
            view = piece(0, side, part)
            pltpu.make_async_copy(view, view, own_sem.at[side, part]).wait()
            forward(0, side, part)
    for copy in loads:
        copy.wait()

    start_row = starts_s[pl.ds(tok, 1), :]
    span = spans_s[tok]
    row_iota = lax.broadcasted_iota(jnp.int32, (QBLOCK, QBLOCK), 0)
    col_iota = lax.broadcasted_iota(jnp.int32, (QBLOCK, QBLOCK), 1)

    def block(slot):
        key = key_win[slot]
        value = value_win[slot]
        key_pos = row_iota + (tok - slot) * QBLOCK
        least = jnp.where(slot < span, start_row, FAR)
        allowed = key_pos >= least
        if slot == 0:
            allowed = allowed & (row_iota <= col_iota)
        value_term = jnp.zeros((QBLOCK, HEAD_DIM), jnp.float32)
        key_term = jnp.zeros((QBLOCK, HEAD_DIM), jnp.float32)
        for pair in range(GROUP // 2):
            block_rows = pl.ds(pair * 2 * QBLOCK, 2 * QBLOCK)
            q_pair = q_s[block_rows, :]
            do_pair = do_s[block_rows, :]
            scores = matmul(key, q_pair, NT)
            prob_grad = matmul(value, do_pair, NT)
            lows, grads = [], []
            for e in range(2):
                h = pair * 2 + e
                lanes = slice(e * QBLOCK, (e + 1) * QBLOCK)
                probs = jnp.where(
                    allowed, jnp.exp(scores[:, lanes] * scale - norm_s[pl.ds(h, 1), :]), 0.0
                )
                lows.append(probs.astype(jnp.bfloat16))
                grads.append(
                    (probs * (prob_grad[:, lanes] - dot_s[pl.ds(h, 1), :])).astype(jnp.bfloat16)
                )
            low = jnp.concatenate(lows, axis=1)
            grad = jnp.concatenate(grads, axis=1)
            ds_all[slot, :, pl.ds(pair * 2 * QBLOCK, 2 * QBLOCK)] = grad
            value_term = value_term + matmul(low, do_pair, NN)
            key_term = key_term + matmul(grad, q_pair, NN)
        key_t[:, pl.ds(slot * QBLOCK, QBLOCK)] = key.T
        return key_term * scale, value_term

    grad_sends = []

    def send_grad(slot, side, step):
        copy = pltpu.make_async_remote_copy(
            src_ref=send_buf.at[slot, side],
            dst_ref=recv_buf.at[slot, side],
            send_sem=grad_send.at[slot, side],
            recv_sem=grad_recv.at[slot, side],
            device_id={"tok": tok_at(-step)},
            device_id_type=MESH,
        )
        copy.start()
        grad_sends.append(copy)
        return copy

    key_term, value_term = block(0)
    own_buf[0] = key_term
    own_buf[1] = value_term
    grads = {}
    for slot in range(1, REACH + 1):
        for side in range(2):
            for part in range(PIECES):
                forwards[((slot - 1) * 2 + side) * PIECES + part].wait_recv()
                if slot < REACH:
                    forward(slot, side, part)
        key_term, value_term = block(slot)
        if slot == REACH - 1:
            far_buf[0] = key_term
            far_buf[1] = value_term
        else:
            send_buf[slot - 1, 0] = key_term.astype(jnp.bfloat16)
            send_buf[slot - 1, 1] = value_term.astype(jnp.bfloat16)
            for side in range(2):
                grads[slot, side] = send_grad(slot - 1, side, 1 if slot == REACH else slot)

    outs = []
    for pair in range(GROUP // 2):
        lanes = pl.ds(pair * 2 * QBLOCK, 2 * QBLOCK)
        grad = ds_all[:, :, lanes].reshape((REACH + 1) * QBLOCK, 2 * QBLOCK)
        dq_t = matmul(key_t[...], grad, NN) * scale
        for e in range(2):
            h = pair * 2 + e
            dq_s[:, pl.ds(h * HEAD_DIM, HEAD_DIM)] = (
                dq_t[:, e * QBLOCK : (e + 1) * QBLOCK].T.astype(jnp.bfloat16)
            )

    for side in range(2):
        grads[REACH, side].wait_recv()
        send_buf[REACH - 2, side] = (
            far_buf[side] + recv_buf[REACH - 1, side].astype(jnp.float32)
        ).astype(jnp.bfloat16)
        grads[REACH - 1, side] = send_grad(REACH - 2, side, REACH - 1)
    copy = pltpu.make_async_copy(dq_s, dq_hbm, out_sem.at[0])
    copy.start()
    outs.append(copy)
    for side in range(2):
        total = own_buf[side]
        for slot in range(1, REACH):
            grads[slot, side].wait_recv()
            total = total + recv_buf[slot - 1, side].astype(jnp.float32)
        out_s[side] = total.astype(jnp.bfloat16)
        copy = pltpu.make_async_copy(out_s.at[side], (dk_hbm, dv_hbm)[side], out_sem.at[1 + side])
        copy.start()
        outs.append(copy)
    for copy in own_copies:
        pass
    for copy in spreads:
        copy.wait_send()
    for copy in forwards:
        copy.wait_send()
    for copy in grad_sends:
        copy.wait_send()
    for copy in outs:
        copy.wait()


def solution(mesh):
    n_tok = mesh.shape["tok"]
    n_head = mesh.shape["head"]
    slots = REACH + 1
    bf16, f32 = jnp.bfloat16, jnp.float32

    def per_device(query, keys, values, out_grad, log_norm, row_dot, doc_start, spans):
        starts = doc_start.reshape(n_tok, QBLOCK)
        anywhere = pl.BlockSpec(memory_space=pl.ANY)
        return pl.pallas_call(
            functools.partial(kernel, n_tok, n_head),
            out_shape=(
                jax.ShapeDtypeStruct((QBLOCK, GROUP * HEAD_DIM), bf16),
                jax.ShapeDtypeStruct((QBLOCK, HEAD_DIM), bf16),
                jax.ShapeDtypeStruct((QBLOCK, HEAD_DIM), bf16),
            ),
            in_specs=[anywhere] * 8,
            out_specs=(anywhere,) * 3,
            scratch_shapes=[
                pltpu.VMEM((GROUP * QBLOCK, HEAD_DIM), bf16),
                pltpu.VMEM((GROUP * QBLOCK, HEAD_DIM), bf16),
                pltpu.VMEM((GROUP, QBLOCK), f32),
                pltpu.VMEM((GROUP, QBLOCK), f32),
                pltpu.VMEM((n_tok, QBLOCK), jnp.int32),
                pltpu.SMEM((n_tok,), jnp.int32),
                pltpu.VMEM((slots, QBLOCK, HEAD_DIM), bf16),
                pltpu.VMEM((slots, QBLOCK, HEAD_DIM), bf16),
                pltpu.VMEM((HEAD_DIM, slots * QBLOCK), bf16),
                pltpu.VMEM((slots, QBLOCK, GROUP * QBLOCK), bf16),
                pltpu.VMEM((REACH, 2, QBLOCK, HEAD_DIM), bf16),
                pltpu.VMEM((REACH, 2, QBLOCK, HEAD_DIM), bf16),
                pltpu.VMEM((2, QBLOCK, HEAD_DIM), f32),
                pltpu.VMEM((2, QBLOCK, HEAD_DIM), f32),
                pltpu.VMEM((QBLOCK, GROUP * HEAD_DIM), bf16),
                pltpu.VMEM((2, QBLOCK, HEAD_DIM), bf16),
                pltpu.SemaphoreType.DMA((2 * GROUP + 4,)),
                pltpu.SemaphoreType.DMA((2, n_head - 1)),
                pltpu.SemaphoreType.DMA((2, PIECES)),
                pltpu.SemaphoreType.DMA((REACH, 2, PIECES)),
                pltpu.SemaphoreType.DMA((REACH, 2, PIECES)),
                pltpu.SemaphoreType.DMA((REACH, 2)),
                pltpu.SemaphoreType.DMA((REACH, 2)),
                pltpu.SemaphoreType.DMA((3,)),
            ],
            compiler_params=pltpu.CompilerParams(collective_id=0, has_side_effects=True),
        )(query, keys, values, out_grad, log_norm, row_dot, starts, spans)

    return jax.shard_map(
        per_device,
        mesh=mesh,
        in_specs=(
            P("tok", "head"),
            P(("tok", "head"), None),
            P(("tok", "head"), None),
            P("tok", "head"),
            P("head", "tok"),
            P("head", "tok"),
            P(),
            P(),
        ),
        out_specs=(P("tok", "head"), P("tok", "head"), P("tok", "head")),
        check_vma=False,
    )
```

```python
import functools
import math

import jax
import jax.numpy as jnp
from jax import lax
from jax.experimental import pallas as pl
from jax.experimental.pallas import tpu as pltpu
from jax.sharding import PartitionSpec as P

HEADS = 64
KV_HEADS = 8
HEAD_DIM = 128
QBLOCK = 128
REACH = 5
GROUP = HEADS // KV_HEADS
PIECES = 2
MESH = pl.DeviceIdType.MESH
FAR = 1 << 30
NS = jax.named_scope

NT = (((1,), (1,)), ((), ()))
NN = (((1,), (0,)), ((), ()))


def matmul(a, b, dims):
    return lax.dot_general(a, b, dims, preferred_element_type=jnp.float32)


def kernel(
    n_tok,
    n_head,
    query_hbm,
    keys_hbm,
    values_hbm,
    outgrad_hbm,
    norm_hbm,
    dot_hbm,
    starts_hbm,
    spans_hbm,
    dq_out,
    dk_out,
    dv_out,
    q_s,
    do_s,
    norm_s,
    dot_s,
    starts_s,
    spans_s,
    key_win,
    value_win,
    key_t,
    ds_all,
    send_buf,
    recv_buf,
    terms,
    in_sem,
    a2a_send,
    own_sem,
    kv_send,
    kv_recv,
    grad_send,
    grad_recv,
):
    scale = 1.0 / math.sqrt(HEAD_DIM)
    tok = lax.axis_index("tok")
    head = lax.axis_index("head")
    rows = QBLOCK // n_head
    half = QBLOCK // PIECES

    def tok_at(step):
        return lax.rem(tok + (step + n_tok), n_tok)

    slot_rows = pl.ds(pl.multiple_of(head * rows, rows), rows)
    my_half = lax.div(head, n_head // PIECES)

    def columns(h):
        return pl.ds(pl.multiple_of(h * HEAD_DIM, HEAD_DIM), HEAD_DIM)

    barrier = pltpu.get_barrier_semaphore()
    for step in range(1, n_head):
        pl.semaphore_signal(
            barrier, 1, device_id={"head": lax.rem(head + step, n_head)}, device_id_type=MESH
        )
    pl.semaphore_signal(barrier, 1, device_id={"tok": tok_at(-1)}, device_id_type=MESH)

    for side, (source, window) in enumerate(((keys_hbm, key_win), (values_hbm, value_win))):
        pltpu.make_async_copy(
            source.at[:, columns(head)], window.at[0, slot_rows, :], own_sem.at[side, my_half]
        ).start()
    loads = []
    for h in range(GROUP):
        block = pl.ds(h * QBLOCK, QBLOCK)
        cols = pl.ds(h * HEAD_DIM, HEAD_DIM)
        loads.append(pltpu.make_async_copy(query_hbm.at[:, cols], q_s.at[block, :], in_sem.at[h]))
        loads.append(
            pltpu.make_async_copy(outgrad_hbm.at[:, cols], do_s.at[block, :], in_sem.at[GROUP + h])
        )
    base = 2 * GROUP
    loads.append(pltpu.make_async_copy(norm_hbm, norm_s, in_sem.at[base]))
    loads.append(pltpu.make_async_copy(dot_hbm, dot_s, in_sem.at[base + 1]))
    loads.append(pltpu.make_async_copy(starts_hbm, starts_s, in_sem.at[base + 2]))
    loads.append(pltpu.make_async_copy(spans_hbm, spans_s, in_sem.at[base + 3]))
    for copy in loads:
        copy.start()
    with NS("xbar"):
        pl.semaphore_wait(barrier, n_head)

    spreads = []
    for side, (source, window) in enumerate(((keys_hbm, key_win), (values_hbm, value_win))):
        for step in range(1, n_head):
            peer = lax.rem(head + step, n_head)
            copy = pltpu.make_async_remote_copy(
                src_ref=source.at[:, columns(peer)],
                dst_ref=window.at[0, slot_rows, :],
                send_sem=a2a_send.at[side, step - 1],
                recv_sem=own_sem.at[side, my_half],
                device_id={"head": peer},
                device_id_type=MESH,
            )
            copy.start()
            spreads.append(copy)

    def piece(slot, side, part):
        window = (key_win, value_win)[side]
        return window.at[slot, pl.ds(part * half, half), :]

    forwards = {}

    def forward(slot, side, part):
        copy = pltpu.make_async_remote_copy(
            src_ref=piece(slot, side, part),
            dst_ref=piece(slot + 1, side, part),
            send_sem=kv_send.at[slot, side, part],
            recv_sem=kv_recv.at[slot, side, part],
            device_id={"tok": tok_at(1)},
            device_id_type=MESH,
        )
        copy.start()
        forwards[slot, side, part] = copy

    pieces = [(side, part) for side in range(2) for part in range(PIECES)]
    for side, part in pieces:
        view = piece(0, side, part)
        with NS(f"xa2a{side}{part}"):
            pltpu.make_async_copy(view, view, own_sem.at[side, part]).wait()
        forward(0, side, part)
    with NS("xloads"):
        for copy in loads:
            copy.wait()

    start_row = starts_s[pl.ds(tok, 1), :]
    span = spans_s[tok]
    row_iota = lax.broadcasted_iota(jnp.int32, (QBLOCK, QBLOCK), 0)
    col_iota = lax.broadcasted_iota(jnp.int32, (QBLOCK, QBLOCK), 1)

    def unit(slot, pair):
        key = key_win[slot]
        value = value_win[slot]
        key_pos = row_iota + (tok - slot) * QBLOCK
        least = jnp.where(slot < span, start_row, FAR)
        allowed = key_pos >= least
        if slot == 0:
            allowed = allowed & (row_iota <= col_iota)
        block_rows = pl.ds(pair * 2 * QBLOCK, 2 * QBLOCK)
        q_pair = q_s[block_rows, :]
        do_pair = do_s[block_rows, :]
        scores = matmul(key, q_pair, NT)
        prob_grad = matmul(value, do_pair, NT)
        lows, grads = [], []
        for e in range(2):
            h = pair * 2 + e
            lanes = slice(e * QBLOCK, (e + 1) * QBLOCK)
            probs = jnp.where(
                allowed, jnp.exp(scores[:, lanes] * scale - norm_s[pl.ds(h, 1), :]), 0.0
            )
            lows.append(probs.astype(jnp.bfloat16))
            grads.append(
                (probs * (prob_grad[:, lanes] - dot_s[pl.ds(h, 1), :])).astype(jnp.bfloat16)
            )
        low = jnp.concatenate(lows, axis=1)
        grad = jnp.concatenate(grads, axis=1)
        ds_all[slot, :, block_rows] = grad
        key_term = matmul(grad, q_pair, NN)
        value_term = matmul(low, do_pair, NN)
        if pair == 0:
            key_t[:, pl.ds(slot * QBLOCK, QBLOCK)] = key.T
            terms[slot, 0] = key_term
            terms[slot, 1] = value_term
        else:
            terms[slot, 0] += key_term
            terms[slot, 1] += value_term

    grads = {}

    def send_grad(slot, side, step, extra=None):
        term = terms[slot, side]
        if side == 0:
            term = term * scale
        if extra is not None:
            term = term + extra
        send_buf[slot - 1, side] = term.astype(jnp.bfloat16)
        copy = pltpu.make_async_remote_copy(
            src_ref=send_buf.at[slot - 1, side],
            dst_ref=recv_buf.at[slot - 1, side],
            send_sem=grad_send.at[slot - 1, side],
            recv_sem=grad_recv.at[slot - 1, side],
            device_id={"tok": tok_at(-step)},
            device_id_type=MESH,
        )
        copy.start()
        grads[slot, side] = copy

    def finish(slot):
        if slot % 2 == 1:
            for side in range(2):
                send_grad(slot, side, 1)

    def join(slot):
        for side in range(2):
            with NS(f"xjoin{slot}{side}"):
                grads[slot + 1, side].wait_recv()
            send_grad(slot, side, slot, recv_buf[slot, side].astype(jnp.float32))

    for slot in range(1, REACH + 1):
        for index, (side, part) in enumerate(pieces):
            with NS(f"xkv{slot}{side}{part}"):
                forwards[slot - 1, side, part].wait_recv()
            if slot < REACH:
                forward(slot, side, part)
            with NS(f"xunit{slot - 1}{index}"):
                unit(slot - 1, index)
        finish(slot - 1)
    with NS("xunit5"):
        for pair in range(GROUP // 2):
            unit(REACH, pair)
    finish(REACH)
    join(2)

    with NS("xdq"):
        for pair in range(GROUP // 2):
            lanes = pl.ds(pair * 2 * QBLOCK, 2 * QBLOCK)
            grad = ds_all[:, :, lanes].reshape((REACH + 1) * QBLOCK, 2 * QBLOCK)
            dq_t = matmul(key_t[...], grad, NN) * scale
            for e in range(2):
                h = pair * 2 + e
                dq_out[:, pl.ds(h * HEAD_DIM, HEAD_DIM)] = (
                    dq_t[:, e * QBLOCK : (e + 1) * QBLOCK].T.astype(jnp.bfloat16)
                )
    join(4)
    for side, out in enumerate((dk_out, dv_out)):
        total = terms[0, side]
        if side == 0:
            total = total * scale
        for slot in (1, 2, 4):
            with NS(f"xgrad{side}{slot}"):
                grads[slot, side].wait_recv()
            total = total + recv_buf[slot - 1, side].astype(jnp.float32)
        out[...] = total.astype(jnp.bfloat16)
    with NS("xsends"):
        for copy in spreads + list(forwards.values()) + list(grads.values()):
            copy.wait_send()


def store(dq_ref, dk_ref, dv_ref, dq_hbm, dk_hbm, dv_hbm, sems):
    copies = [
        pltpu.make_async_copy(source, target, sems.at[index])
        for index, (source, target) in enumerate(
            ((dq_ref, dq_hbm), (dk_ref, dk_hbm), (dv_ref, dv_hbm))
        )
    ]
    for copy in copies:
        copy.start()
    for copy in copies:
        copy.wait()


def solution(mesh):
    n_tok = mesh.shape["tok"]
    n_head = mesh.shape["head"]
    slots = REACH + 1
    bf16, f32 = jnp.bfloat16, jnp.float32

    def per_device(query, keys, values, out_grad, log_norm, row_dot, doc_start, spans):
        starts = doc_start.reshape(n_tok, QBLOCK)
        anywhere = pl.BlockSpec(memory_space=pl.ANY)
        outside = pl.BlockSpec(memory_space=pltpu.HBM)
        inside = pl.BlockSpec(memory_space=pltpu.VMEM)
        shapes = (
            jax.ShapeDtypeStruct((QBLOCK, GROUP * HEAD_DIM), bf16),
            jax.ShapeDtypeStruct((QBLOCK, HEAD_DIM), bf16),
            jax.ShapeDtypeStruct((QBLOCK, HEAD_DIM), bf16),
        )
        grads = pl.pallas_call(
            functools.partial(kernel, n_tok, n_head),
            out_shape=tuple(pltpu.VMEM(shape.shape, shape.dtype) for shape in shapes),
            in_specs=[outside] * 8,
            out_specs=(inside,) * 3,
            scratch_shapes=[
                pltpu.VMEM((GROUP * QBLOCK, HEAD_DIM), bf16),
                pltpu.VMEM((GROUP * QBLOCK, HEAD_DIM), bf16),
                pltpu.VMEM((GROUP, QBLOCK), f32),
                pltpu.VMEM((GROUP, QBLOCK), f32),
                pltpu.VMEM((n_tok, QBLOCK), jnp.int32),
                pltpu.SMEM((n_tok,), jnp.int32),
                pltpu.VMEM((slots, QBLOCK, HEAD_DIM), bf16),
                pltpu.VMEM((slots, QBLOCK, HEAD_DIM), bf16),
                pltpu.VMEM((HEAD_DIM, slots * QBLOCK), bf16),
                pltpu.VMEM((slots, QBLOCK, GROUP * QBLOCK), bf16),
                pltpu.VMEM((REACH, 2, QBLOCK, HEAD_DIM), bf16),
                pltpu.VMEM((REACH, 2, QBLOCK, HEAD_DIM), bf16),
                pltpu.VMEM((slots, 2, QBLOCK, HEAD_DIM), f32),
                pltpu.SemaphoreType.DMA((2 * GROUP + 4,)),
                pltpu.SemaphoreType.DMA((2, n_head - 1)),
                pltpu.SemaphoreType.DMA((2, PIECES)),
                pltpu.SemaphoreType.DMA((REACH, 2, PIECES)),
                pltpu.SemaphoreType.DMA((REACH, 2, PIECES)),
                pltpu.SemaphoreType.DMA((REACH, 2)),
                pltpu.SemaphoreType.DMA((REACH, 2)),
            ],
            compiler_params=pltpu.CompilerParams(
                collective_id=0, has_side_effects=True
            ),
        )(query, keys, values, out_grad, log_norm, row_dot, starts, spans)
        return pl.pallas_call(
            store,
            out_shape=shapes,
            in_specs=[inside] * 3,
            out_specs=(anywhere,) * 3,
            scratch_shapes=[pltpu.SemaphoreType.DMA((3,))],
            compiler_params=pltpu.CompilerParams(vmem_limit_bytes=4 << 20),
        )(*grads)

    return jax.shard_map(
        per_device,
        mesh=mesh,
        in_specs=(
            P("tok", "head"),
            P(("tok", "head"), None),
            P(("tok", "head"), None),
            P("tok", "head"),
            P("head", "tok"),
            P("head", "tok"),
            P(),
            P(),
        ),
        out_specs=(P("tok", "head"), P("tok", "head"), P("tok", "head")),
        check_vma=False,
    )
```

```python
import functools
import math

import jax
import jax.numpy as jnp
from jax import lax
from jax.experimental import pallas as pl
from jax.experimental.pallas import tpu as pltpu
from jax.sharding import PartitionSpec as P

HEADS = 64
KV_HEADS = 8
HEAD_DIM = 128
QBLOCK = 128
REACH = 5
GROUP = HEADS // KV_HEADS
PIECES = 2
MESH = pl.DeviceIdType.MESH
FAR = 1 << 30
NS = jax.named_scope
JOIN = 3
ROW = 32
SPLIT = True

NT = (((1,), (1,)), ((), ()))
NN = (((1,), (0,)), ((), ()))


def matmul(a, b, dims):
    return lax.dot_general(a, b, dims, preferred_element_type=jnp.float32)


def kernel(
    n_tok,
    n_head,
    query_hbm,
    keys_hbm,
    values_hbm,
    outgrad_hbm,
    norm_hbm,
    dot_hbm,
    starts_hbm,
    spans_hbm,
    dq_out,
    dk_out,
    dv_out,
    keys_s,
    values_s,
    q_s,
    do_s,
    norm_s,
    dot_s,
    starts_s,
    spans_s,
    key_win,
    value_win,
    key_t,
    ds_all,
    send_buf,
    recv_buf,
    join_buf,
    terms,
    stage_sem,
    in_sem,
    a2a_send,
    own_sem,
    kv_send,
    kv_recv,
    grad_send,
    grad_recv,
    join_recv,
    leap_send,
):
    scale = 1.0 / math.sqrt(HEAD_DIM)
    tok = lax.axis_index("tok")
    head = lax.axis_index("head")
    rows = QBLOCK // n_head
    half = QBLOCK // PIECES

    place = lax.rem(tok, ROW)
    ahead = ROW - place
    crosses = (ahead == REACH) & (tok + ahead < n_tok)

    def tok_at(step):
        return lax.rem(tok + (step + n_tok), n_tok)

    slot_rows = pl.ds(pl.multiple_of(head * rows, rows), rows)
    my_half = lax.div(head, n_head // PIECES)

    def columns(h):
        return pl.ds(pl.multiple_of(h * HEAD_DIM, HEAD_DIM), HEAD_DIM)

    barrier = pltpu.get_barrier_semaphore()
    with NS("xsig"):
        for step in range(1, n_head):
            pl.semaphore_signal(
                barrier, 1, device_id={"head": lax.rem(head + step, n_head)}, device_id_type=MESH
            )

        @pl.when(tok > 0)
        def _():
            pl.semaphore_signal(barrier, 1, device_id={"tok": tok_at(-1)}, device_id_type=MESH)

        if SPLIT:

            @pl.when((place == 0) & (tok > 0))
            def _():
                pl.semaphore_signal(
                    barrier, 1, device_id={"tok": tok_at(-REACH)}, device_id_type=MESH
                )


    sides = ((keys_hbm, keys_s, key_win), (values_hbm, values_s, value_win))
    with NS("xld"):
        stages = []
        for side, (source, stage, window) in enumerate(sides):
            pltpu.make_async_copy(
                source.at[:, columns(head)], window.at[0, slot_rows, :], own_sem.at[side, my_half]
            ).start()
            stages.append(pltpu.make_async_copy(source, stage, stage_sem.at[side]))
            stages[-1].start()
        loads = []
        for h in range(GROUP):
            block = pl.ds(h * QBLOCK, QBLOCK)
            cols = pl.ds(h * HEAD_DIM, HEAD_DIM)
            loads.append(
                pltpu.make_async_copy(query_hbm.at[:, cols], q_s.at[block, :], in_sem.at[h])
            )
            loads.append(
                pltpu.make_async_copy(
                    outgrad_hbm.at[:, cols], do_s.at[block, :], in_sem.at[GROUP + h]
                )
            )
        base = 2 * GROUP
        loads.append(pltpu.make_async_copy(norm_hbm, norm_s, in_sem.at[base]))
        loads.append(pltpu.make_async_copy(dot_hbm, dot_s, in_sem.at[base + 1]))
        loads.append(pltpu.make_async_copy(starts_hbm, starts_s, in_sem.at[base + 2]))
        loads.append(pltpu.make_async_copy(spans_hbm, spans_s, in_sem.at[base + 3]))
        for copy in loads:
            copy.start()
    with NS("xstage"):
        for copy in stages:
            copy.wait()
    with NS("xbar"):
        waits = n_head - 1 + jnp.where(tok + 1 < n_tok, 1, 0)
        if SPLIT:
            waits = waits + jnp.where(crosses, 1, 0)
        pl.semaphore_wait(barrier, waits)

    spreads = []
    with NS("xspread"):
        for side, (_, stage, window) in enumerate(sides):
            for step in range(1, n_head):
                peer = lax.rem(head + step, n_head)
                copy = pltpu.make_async_remote_copy(
                    src_ref=stage.at[:, columns(peer)],
                    dst_ref=window.at[0, slot_rows, :],
                    send_sem=a2a_send.at[side, step - 1],
                    recv_sem=own_sem.at[side, my_half],
                    device_id={"head": peer},
                    device_id_type=MESH,
                )
                copy.start()
                spreads.append(copy)

    def piece(slot, side, part):
        window = (key_win, value_win)[side]
        return window.at[slot, pl.ds(part * half, half), :]

    def forward(slot, side, part):
        return pltpu.make_async_remote_copy(
            src_ref=piece(slot, side, part),
            dst_ref=piece(slot + 1, side, part),
            send_sem=kv_send.at[slot, side, part],
            recv_sem=kv_recv.at[slot, side, part],
            device_id={"tok": tok_at(1)},
            device_id_type=MESH,
        )

    def leap(side, part):
        return pltpu.make_async_remote_copy(
            src_ref=piece(0, side, part),
            dst_ref=piece(REACH, side, part),
            send_sem=leap_send.at[side, part],
            recv_sem=kv_recv.at[REACH - 1, side, part],
            device_id={"tok": tok_at(REACH)},
            device_id_type=MESH,
        )

    def forwards(slot):
        if SPLIT and slot == REACH - 1:
            return (tok >= slot) & (place != ROW - 1)
        return (tok >= slot) & (tok + 1 < n_tok)

    pieces = [(side, part) for side in range(2) for part in range(PIECES)]
    for side, part in pieces:
        view = piece(0, side, part)
        with NS(f"xa2a{side}{part}"):
            pltpu.make_async_copy(view, view, own_sem.at[side, part]).wait()
        if SPLIT:

            @pl.when(crosses)
            def _():
                leap(side, part).start()

        @pl.when(forwards(0))
        def _():
            forward(0, side, part).start()

    with NS("xloads"):
        for copy in loads:
            copy.wait()

    start_row = starts_s[pl.ds(tok, 1), :]
    span = spans_s[tok]
    row_iota = lax.broadcasted_iota(jnp.int32, (QBLOCK, QBLOCK), 0)
    col_iota = lax.broadcasted_iota(jnp.int32, (QBLOCK, QBLOCK), 1)

    def block(slot):
        key = key_win[slot]
        value = value_win[slot]
        key_pos = row_iota + (tok - slot) * QBLOCK
        least = jnp.where(slot < span, start_row, FAR)
        allowed = key_pos >= least
        if slot == 0:
            allowed = allowed & (row_iota <= col_iota)
        value_term = jnp.zeros((QBLOCK, HEAD_DIM), jnp.float32)
        key_term = jnp.zeros((QBLOCK, HEAD_DIM), jnp.float32)
        for pair in range(GROUP // 2):
            block_rows = pl.ds(pair * 2 * QBLOCK, 2 * QBLOCK)
            q_pair = q_s[block_rows, :]
            do_pair = do_s[block_rows, :]
            scores = matmul(key, q_pair, NT)
            prob_grad = matmul(value, do_pair, NT)
            lows, grads = [], []
            for e in range(2):
                h = pair * 2 + e
                lanes = slice(e * QBLOCK, (e + 1) * QBLOCK)
                probs = jnp.where(
                    allowed, jnp.exp(scores[:, lanes] * scale - norm_s[pl.ds(h, 1), :]), 0.0
                )
                lows.append(probs.astype(jnp.bfloat16))
                grads.append(
                    (probs * (prob_grad[:, lanes] - dot_s[pl.ds(h, 1), :])).astype(jnp.bfloat16)
                )
            low = jnp.concatenate(lows, axis=1)
            grad = jnp.concatenate(grads, axis=1)
            ds_all[slot, :, block_rows] = grad
            value_term = value_term + matmul(low, do_pair, NN)
            key_term = key_term + matmul(grad, q_pair, NN)
        key_t[:, pl.ds(slot * QBLOCK, QBLOCK)] = key.T
        return key_term * scale, value_term

    def home(slot):
        return pltpu.make_async_remote_copy(
            src_ref=send_buf.at[slot - 1],
            dst_ref=recv_buf.at[slot - 1],
            send_sem=grad_send.at[slot - 1],
            recv_sem=grad_recv.at[slot - 1],
            device_id={"tok": tok_at(-slot)},
            device_id_type=MESH,
        )

    def onward(slot):
        return pltpu.make_async_remote_copy(
            src_ref=send_buf.at[slot - 1],
            dst_ref=join_buf.at[slot - 1],
            send_sem=grad_send.at[slot - 1],
            recv_sem=join_recv.at[slot - 1],
            device_id={"tok": tok_at(1)},
            device_id_type=MESH,
        )

    def goes_on(slot):
        if slot < JOIN or slot == REACH:
            return False
        return (place != ROW - 1) if SPLIT else (tok + 1 < n_tok)

    def joins(slot):
        if slot <= JOIN:
            return False
        return ((place != 0) if SPLIT else (tok > 0)) & (tok >= slot)

    def compute(slot):
        with NS(f"xblock{slot}"):
            both = block(slot)
            for side in range(2):
                terms[slot, side] = both[side]

    def ship(slot):
        with NS(f"xship{slot}"):
            if joins(slot) is False:
                for side in range(2):
                    send_buf[slot - 1, side] = terms[slot, side].astype(jnp.bfloat16)
            else:

                @pl.when(joins(slot))
                def _():
                    onward(slot - 1).wait_recv()
                    for side in range(2):
                        send_buf[slot - 1, side] = (
                            terms[slot, side] + join_buf[slot - 2, side].astype(jnp.float32)
                        ).astype(jnp.bfloat16)

                @pl.when(jnp.logical_not(joins(slot)))
                def _():
                    for side in range(2):
                        send_buf[slot - 1, side] = terms[slot, side].astype(jnp.bfloat16)

            passing = goes_on(slot)
            if passing is False:
                home(slot).start()
            else:

                @pl.when(passing)
                def _():
                    onward(slot).start()

                @pl.when(jnp.logical_not(passing))
                def _():
                    if SPLIT:
                        home(slot).start()

    def arrive(slot):
        for side, part in pieces:
            with NS(f"xkv{slot}{side}{part}"):
                forward(slot - 1, side, part).wait_recv()
            if slot < REACH:

                @pl.when(forwards(slot))
                def _():
                    forward(slot, side, part).start()

    compute(0)
    for slot in range(1, REACH + 1):

        @pl.when(tok >= slot)
        def _():
            arrive(slot)
            compute(slot)
            if slot < REACH:
                ship(slot)

        @pl.when(tok < slot)
        def _():
            ds_all[slot] = jnp.zeros((QBLOCK, GROUP * QBLOCK), jnp.bfloat16)
            key_t[:, pl.ds(slot * QBLOCK, QBLOCK)] = jnp.zeros((HEAD_DIM, QBLOCK), jnp.bfloat16)

    with NS("xdq"):
        for pair in range(GROUP // 2):
            lanes = pl.ds(pair * 2 * QBLOCK, 2 * QBLOCK)
            grad = ds_all[:, :, lanes].reshape((REACH + 1) * QBLOCK, 2 * QBLOCK)
            dq_t = matmul(key_t[...], grad, NN) * scale
            for e in range(2):
                h = pair * 2 + e
                dq_out[:, pl.ds(h * HEAD_DIM, HEAD_DIM)] = (
                    dq_t[:, e * QBLOCK : (e + 1) * QBLOCK].T.astype(jnp.bfloat16)
                )

    @pl.when(tok >= REACH)
    def _():
        ship(REACH)

    for slot in range(1, REACH + 1):
        expected = tok + slot < n_tok
        if JOIN <= slot < REACH:
            if not SPLIT:
                continue
            expected = place + slot == ROW - 1
        with NS(f"xgrad{slot}"):

            @pl.when(expected)
            def _():
                home(slot).wait_recv()
                for side in range(2):
                    terms[0, side] += recv_buf[slot - 1, side].astype(jnp.float32)

    for side, out in enumerate((dk_out, dv_out)):
        out[...] = terms[0, side].astype(jnp.bfloat16)
    with NS("xsends"):
        for copy in spreads:
            copy.wait_send()
        for side, part in pieces:
            if SPLIT:

                @pl.when(crosses)
                def _():
                    leap(side, part).wait_send()

        for slot in range(REACH):

            @pl.when(forwards(slot))
            def _():
                for side, part in pieces:
                    forward(slot, side, part).wait_send()

    with NS("xsendg"):
        for slot in range(1, REACH + 1):

            @pl.when(tok >= slot)
            def _():
                home(slot).wait_send()


def store(dq_ref, dk_ref, dv_ref, dq_hbm, dk_hbm, dv_hbm, sems):
    copies = [
        pltpu.make_async_copy(source, target, sems.at[index])
        for index, (source, target) in enumerate(
            ((dq_ref, dq_hbm), (dk_ref, dk_hbm), (dv_ref, dv_hbm))
        )
    ]
    for copy in copies:
        copy.start()
    for copy in copies:
        copy.wait()


def solution(mesh):
    n_tok = mesh.shape["tok"]
    n_head = mesh.shape["head"]
    slots = REACH + 1
    bf16, f32 = jnp.bfloat16, jnp.float32

    def per_device(query, keys, values, out_grad, log_norm, row_dot, doc_start, spans):
        starts = doc_start.reshape(n_tok, QBLOCK)
        anywhere = pl.BlockSpec(memory_space=pl.ANY)
        outside = pl.BlockSpec(memory_space=pltpu.HBM)
        inside = pl.BlockSpec(memory_space=pltpu.VMEM)
        shapes = (
            jax.ShapeDtypeStruct((QBLOCK, GROUP * HEAD_DIM), bf16),
            jax.ShapeDtypeStruct((QBLOCK, HEAD_DIM), bf16),
            jax.ShapeDtypeStruct((QBLOCK, HEAD_DIM), bf16),
        )
        grads = pl.pallas_call(
            functools.partial(kernel, n_tok, n_head),
            out_shape=tuple(pltpu.VMEM(shape.shape, shape.dtype) for shape in shapes),
            in_specs=[outside] * 8,
            out_specs=(inside,) * 3,
            scratch_shapes=[
                pltpu.VMEM((QBLOCK // n_head, KV_HEADS * HEAD_DIM), bf16),
                pltpu.VMEM((QBLOCK // n_head, KV_HEADS * HEAD_DIM), bf16),
                pltpu.VMEM((GROUP * QBLOCK, HEAD_DIM), bf16),
                pltpu.VMEM((GROUP * QBLOCK, HEAD_DIM), bf16),
                pltpu.VMEM((GROUP, QBLOCK), f32),
                pltpu.VMEM((GROUP, QBLOCK), f32),
                pltpu.VMEM((n_tok, QBLOCK), jnp.int32),
                pltpu.SMEM((n_tok,), jnp.int32),
                pltpu.VMEM((slots, QBLOCK, HEAD_DIM), bf16),
                pltpu.VMEM((slots, QBLOCK, HEAD_DIM), bf16),
                pltpu.VMEM((HEAD_DIM, slots * QBLOCK), bf16),
                pltpu.VMEM((slots, QBLOCK, GROUP * QBLOCK), bf16),
                pltpu.VMEM((REACH, 2, QBLOCK, HEAD_DIM), bf16),
                pltpu.VMEM((REACH, 2, QBLOCK, HEAD_DIM), bf16),
                pltpu.VMEM((REACH, 2, QBLOCK, HEAD_DIM), bf16),
                pltpu.VMEM((slots, 2, QBLOCK, HEAD_DIM), f32),
                pltpu.SemaphoreType.DMA((2,)),
                pltpu.SemaphoreType.DMA((2 * GROUP + 4,)),
                pltpu.SemaphoreType.DMA((2, n_head - 1)),
                pltpu.SemaphoreType.DMA((2, PIECES)),
                pltpu.SemaphoreType.DMA((REACH, 2, PIECES)),
                pltpu.SemaphoreType.DMA((REACH, 2, PIECES)),
                pltpu.SemaphoreType.DMA((REACH,)),
                pltpu.SemaphoreType.DMA((REACH,)),
                pltpu.SemaphoreType.DMA((REACH,)),
                pltpu.SemaphoreType.DMA((2, PIECES)),
            ],
            compiler_params=pltpu.CompilerParams(
                collective_id=0, has_side_effects=True
            ),
        )(query, keys, values, out_grad, log_norm, row_dot, starts, spans)
        return pl.pallas_call(
            store,
            out_shape=shapes,
            in_specs=[inside] * 3,
            out_specs=(anywhere,) * 3,
            scratch_shapes=[pltpu.SemaphoreType.DMA((3,))],
            compiler_params=pltpu.CompilerParams(vmem_limit_bytes=4 << 20),
        )(*grads)

    return jax.shard_map(
        per_device,
        mesh=mesh,
        in_specs=(
            P("tok", "head"),
            P(("tok", "head"), None),
            P(("tok", "head"), None),
            P("tok", "head"),
            P("head", "tok"),
            P("head", "tok"),
            P(),
            P(),
        ),
        out_specs=(P("tok", "head"), P("tok", "head"), P("tok", "head")),
        check_vma=False,
    )
```

```python
import functools
import math

import jax
import jax.numpy as jnp
from jax import lax
from jax.experimental import pallas as pl
from jax.experimental.pallas import tpu as pltpu
from jax.sharding import PartitionSpec as P

HEADS = 64
KV_HEADS = 8
HEAD_DIM = 128
QBLOCK = 128
REACH = 5
GROUP = HEADS // KV_HEADS
PIECES = 4
MESH = pl.DeviceIdType.MESH
FAR = 1 << 30
NS = jax.named_scope
JOIN = 3
ROW = 32

NT = (((1,), (1,)), ((), ()))
NN = (((1,), (0,)), ((), ()))


def matmul(a, b, dims):
    return lax.dot_general(a, b, dims, preferred_element_type=jnp.float32)


def kernel(
    n_tok,
    n_head,
    query_hbm,
    keys_hbm,
    values_hbm,
    outgrad_hbm,
    norm_hbm,
    dot_hbm,
    starts_hbm,
    spans_hbm,
    dq_out,
    dk_out,
    dv_out,
    keys_s,
    values_s,
    q_s,
    do_s,
    norm_s,
    dot_s,
    starts_s,
    spans_s,
    key_win,
    value_win,
    key_t,
    ds_all,
    send_buf,
    recv_buf,
    join_buf,
    terms,
    stage_sem,
    in_sem,
    a2a_send,
    own_sem,
    kv_send,
    kv_recv,
    grad_send,
    grad_recv,
    join_recv,
    next_send,
    turn,
):
    scale = 1.0 / math.sqrt(HEAD_DIM)
    tok = lax.axis_index("tok")
    head = lax.axis_index("head")
    rows = QBLOCK // n_head
    half = QBLOCK // PIECES

    place = lax.rem(tok, ROW)

    def tok_at(step):
        return lax.rem(tok + (step + n_tok), n_tok)

    slot_rows = pl.ds(pl.multiple_of(head * rows, rows), rows)
    my_half = lax.div(head, n_head // PIECES)

    def columns(h):
        return pl.ds(pl.multiple_of(h * HEAD_DIM, HEAD_DIM), HEAD_DIM)

    barrier = pltpu.get_barrier_semaphore()
    with NS("xsig"):
        for step in range(1, n_head):
            pl.semaphore_signal(
                barrier, 1, device_id={"head": lax.rem(head + step, n_head)}, device_id_type=MESH
            )

        @pl.when(tok > 0)
        def _():
            for step in range(n_head):
                pl.semaphore_signal(
                    barrier,
                    1,
                    device_id={"tok": tok_at(-1), "head": lax.rem(head + step, n_head)},
                    device_id_type=MESH,
                )

    sides = ((keys_hbm, keys_s, key_win), (values_hbm, values_s, value_win))
    with NS("xld"):
        stages = []
        for side, (source, stage, window) in enumerate(sides):
            pltpu.make_async_copy(
                source.at[:, columns(head)], window.at[0, slot_rows, :], own_sem.at[side, my_half]
            ).start()
            stages.append(pltpu.make_async_copy(source, stage, stage_sem.at[side]))
            stages[-1].start()
        loads = []
        for h in range(GROUP):
            block = pl.ds(h * QBLOCK, QBLOCK)
            cols = pl.ds(h * HEAD_DIM, HEAD_DIM)
            loads.append(
                pltpu.make_async_copy(query_hbm.at[:, cols], q_s.at[block, :], in_sem.at[h])
            )
            loads.append(
                pltpu.make_async_copy(
                    outgrad_hbm.at[:, cols], do_s.at[block, :], in_sem.at[GROUP + h]
                )
            )
        base = 2 * GROUP
        loads.append(pltpu.make_async_copy(norm_hbm, norm_s, in_sem.at[base]))
        loads.append(pltpu.make_async_copy(dot_hbm, dot_s, in_sem.at[base + 1]))
        loads.append(pltpu.make_async_copy(starts_hbm, starts_s, in_sem.at[base + 2]))
        loads.append(pltpu.make_async_copy(spans_hbm, spans_s, in_sem.at[base + 3]))
        for copy in loads:
            copy.start()
    with NS("xstage"):
        for copy in stages:
            copy.wait()
    with NS("xbar"):
        waits = n_head - 1 + jnp.where(tok + 1 < n_tok, n_head, 0)
        pl.semaphore_wait(barrier, waits)

    def to_next(side, step):
        _, stage, window = sides[side]
        peer = lax.rem(head + step, n_head)
        return pltpu.make_async_remote_copy(
            src_ref=stage.at[:, columns(peer)],
            dst_ref=window.at[1, slot_rows, :],
            send_sem=next_send.at[side, step],
            recv_sem=kv_recv.at[0, side, my_half],
            device_id={"tok": tok_at(1), "head": peer},
            device_id_type=MESH,
        )

    spreads = []
    with NS("xspread"):
        for side, (_, stage, window) in enumerate(sides):

            @pl.when(tok + 1 < n_tok)
            def _():
                for step in range(n_head):
                    to_next(side, step).start()

        for side, (_, stage, window) in enumerate(sides):
            for step in range(1, n_head):
                peer = lax.rem(head + step, n_head)
                copy = pltpu.make_async_remote_copy(
                    src_ref=stage.at[:, columns(peer)],
                    dst_ref=window.at[0, slot_rows, :],
                    send_sem=a2a_send.at[side, step - 1],
                    recv_sem=own_sem.at[side, my_half],
                    device_id={"head": peer},
                    device_id_type=MESH,
                )
                copy.start()
                spreads.append(copy)

    def piece(slot, side, part):
        window = (key_win, value_win)[side]
        return window.at[slot, pl.ds(part * half, half), :]

    def forward(slot, side, part):
        return pltpu.make_async_remote_copy(
            src_ref=piece(slot, side, part),
            dst_ref=piece(slot + 1, side, part),
            send_sem=kv_send.at[slot, side, part],
            recv_sem=kv_recv.at[slot, side, part],
            device_id={"tok": tok_at(1)},
            device_id_type=MESH,
        )

    def forwards(slot):
        return (tok >= slot) & (tok + 1 < n_tok)

    pieces = [(side, part) for side in range(2) for part in range(PIECES)]
    for side, part in pieces:
        view = piece(0, side, part)
        with NS(f"xa2a{side}{part}"):
            pltpu.make_async_copy(view, view, own_sem.at[side, part]).wait()

    with NS("xloads"):
        for copy in loads:
            copy.wait()

    start_row = starts_s[pl.ds(tok, 1), :]
    span = spans_s[tok]
    row_iota = lax.broadcasted_iota(jnp.int32, (QBLOCK, QBLOCK), 0)
    col_iota = lax.broadcasted_iota(jnp.int32, (QBLOCK, QBLOCK), 1)

    def block(slot):
        key = key_win[slot]
        value = value_win[slot]
        key_pos = row_iota + (tok - slot) * QBLOCK
        least = jnp.where(slot < span, start_row, FAR)
        allowed = key_pos >= least
        if slot == 0:
            allowed = allowed & (row_iota <= col_iota)
        value_term = jnp.zeros((QBLOCK, HEAD_DIM), jnp.float32)
        key_term = jnp.zeros((QBLOCK, HEAD_DIM), jnp.float32)
        for pair in range(GROUP // 2):
            block_rows = pl.ds(pair * 2 * QBLOCK, 2 * QBLOCK)
            q_pair = q_s[block_rows, :]
            do_pair = do_s[block_rows, :]
            scores = matmul(key, q_pair, NT)
            prob_grad = matmul(value, do_pair, NT)
            lows, grads = [], []
            for e in range(2):
                h = pair * 2 + e
                lanes = slice(e * QBLOCK, (e + 1) * QBLOCK)
                probs = jnp.where(
                    allowed, jnp.exp(scores[:, lanes] * scale - norm_s[pl.ds(h, 1), :]), 0.0
                )
                lows.append(probs.astype(jnp.bfloat16))
                grads.append(
                    (probs * (prob_grad[:, lanes] - dot_s[pl.ds(h, 1), :])).astype(jnp.bfloat16)
                )
            low = jnp.concatenate(lows, axis=1)
            grad = jnp.concatenate(grads, axis=1)
            ds_all[slot, :, block_rows] = grad
            value_term = value_term + matmul(low, do_pair, NN)
            key_term = key_term + matmul(grad, q_pair, NN)
        key_t[:, pl.ds(slot * QBLOCK, QBLOCK)] = key.T
        return key_term * scale, value_term

    def home(slot):
        return pltpu.make_async_remote_copy(
            src_ref=send_buf.at[slot - 1],
            dst_ref=recv_buf.at[slot - 1],
            send_sem=grad_send.at[slot - 1],
            recv_sem=grad_recv.at[slot - 1],
            device_id={"tok": tok_at(-slot)},
            device_id_type=MESH,
        )

    def onward(slot):
        return pltpu.make_async_remote_copy(
            src_ref=send_buf.at[slot - 1],
            dst_ref=join_buf.at[slot - 1],
            send_sem=grad_send.at[slot - 1],
            recv_sem=join_recv.at[slot - 1],
            device_id={"tok": tok_at(1)},
            device_id_type=MESH,
        )

    def goes_on(slot):
        if slot < JOIN or slot == REACH:
            return False
        return place != ROW - 1

    def joins(slot):
        if slot <= JOIN:
            return False
        return (place != 0) & (tok >= slot)

    def compute(slot):
        with NS(f"xblock{slot}"):
            both = block(slot)
            for side in range(2):
                terms[slot, side] = both[side]

    def ship(slot):
        with NS(f"xship{slot}"):
            if joins(slot) is False:
                for side in range(2):
                    send_buf[slot - 1, side] = terms[slot, side].astype(jnp.bfloat16)
            else:

                @pl.when(joins(slot))
                def _():
                    onward(slot - 1).wait_recv()
                    for side in range(2):
                        send_buf[slot - 1, side] = (
                            terms[slot, side] + join_buf[slot - 2, side].astype(jnp.float32)
                        ).astype(jnp.bfloat16)

                @pl.when(jnp.logical_not(joins(slot)))
                def _():
                    for side in range(2):
                        send_buf[slot - 1, side] = terms[slot, side].astype(jnp.bfloat16)

            passing = goes_on(slot)
            if passing is False:
                home(slot).start()
            else:

                @pl.when(passing)
                def _():
                    onward(slot).start()

                @pl.when(jnp.logical_not(passing))
                def _():
                    home(slot).start()

    def arrive(slot):
        for side, part in pieces:
            with NS(f"xkv{slot}{side}{part}"):
                view = piece(slot, side, part)
                pltpu.make_async_copy(view, view, kv_recv.at[slot - 1, side, part]).wait()
            if slot < REACH:

                @pl.when(forwards(slot))
                def _():
                    forward(slot, side, part).start()

    compute(0)
    for slot in range(1, REACH + 1):

        @pl.when(tok >= slot)
        def _():
            arrive(slot)
            compute(slot)
            if slot < REACH:
                ship(slot)

        @pl.when(tok < slot)
        def _():
            ds_all[slot] = jnp.zeros((QBLOCK, GROUP * QBLOCK), jnp.bfloat16)
            key_t[:, pl.ds(slot * QBLOCK, QBLOCK)] = jnp.zeros((HEAD_DIM, QBLOCK), jnp.bfloat16)

    early = (place == 0) & (tok >= REACH)

    crossing = (place < REACH) & (tok >= ROW)

    def pass_turn():
        @pl.when(crossing & (place < REACH - 1))
        def _():
            pl.semaphore_signal(turn, 1, device_id={"tok": tok_at(1)}, device_id_type=MESH)

    @pl.when(early)
    def _():
        ship(REACH)
        pass_turn()

    with NS("xdq"):
        for pair in range(GROUP // 2):
            lanes = pl.ds(pair * 2 * QBLOCK, 2 * QBLOCK)
            grad = ds_all[:, :, lanes].reshape((REACH + 1) * QBLOCK, 2 * QBLOCK)
            dq_t = matmul(key_t[...], grad, NN) * scale
            for e in range(2):
                h = pair * 2 + e
                dq_out[:, pl.ds(h * HEAD_DIM, HEAD_DIM)] = (
                    dq_t[:, e * QBLOCK : (e + 1) * QBLOCK].T.astype(jnp.bfloat16)
                )

    @pl.when((tok >= REACH) & jnp.logical_not(early))
    def _():
        @pl.when(crossing)
        def _():
            pl.semaphore_wait(turn, 1)

        ship(REACH)
        pass_turn()

    for slot in range(1, REACH + 1):
        expected = tok + slot < n_tok
        if JOIN <= slot < REACH:
            expected = place + slot == ROW - 1
        with NS(f"xgrad{slot}"):

            @pl.when(expected)
            def _():
                home(slot).wait_recv()
                for side in range(2):
                    terms[0, side] += recv_buf[slot - 1, side].astype(jnp.float32)

    for side, out in enumerate((dk_out, dv_out)):
        out[...] = terms[0, side].astype(jnp.bfloat16)
    with NS("xsends"):
        for copy in spreads:
            copy.wait_send()
        @pl.when(tok + 1 < n_tok)
        def _():
            for side in range(2):
                for step in range(n_head):
                    to_next(side, step).wait_send()

        for slot in range(1, REACH):

            @pl.when(forwards(slot))
            def _():
                for side, part in pieces:
                    forward(slot, side, part).wait_send()

    with NS("xsendg"):
        for slot in range(1, REACH + 1):

            @pl.when(tok >= slot)
            def _():
                home(slot).wait_send()


def store(dq_ref, dk_ref, dv_ref, dq_hbm, dk_hbm, dv_hbm, sems):
    copies = [
        pltpu.make_async_copy(source, target, sems.at[index])
        for index, (source, target) in enumerate(
            ((dq_ref, dq_hbm), (dk_ref, dk_hbm), (dv_ref, dv_hbm))
        )
    ]
    for copy in copies:
        copy.start()
    for copy in copies:
        copy.wait()


def solution(mesh):
    n_tok = mesh.shape["tok"]
    n_head = mesh.shape["head"]
    slots = REACH + 1
    bf16, f32 = jnp.bfloat16, jnp.float32

    def per_device(query, keys, values, out_grad, log_norm, row_dot, doc_start, spans):
        starts = doc_start.reshape(n_tok, QBLOCK)
        anywhere = pl.BlockSpec(memory_space=pl.ANY)
        outside = pl.BlockSpec(memory_space=pltpu.HBM)
        inside = pl.BlockSpec(memory_space=pltpu.VMEM)
        shapes = (
            jax.ShapeDtypeStruct((QBLOCK, GROUP * HEAD_DIM), bf16),
            jax.ShapeDtypeStruct((QBLOCK, HEAD_DIM), bf16),
            jax.ShapeDtypeStruct((QBLOCK, HEAD_DIM), bf16),
        )
        grads = pl.pallas_call(
            functools.partial(kernel, n_tok, n_head),
            out_shape=tuple(pltpu.VMEM(shape.shape, shape.dtype) for shape in shapes),
            in_specs=[outside] * 8,
            out_specs=(inside,) * 3,
            scratch_shapes=[
                pltpu.VMEM((QBLOCK // n_head, KV_HEADS * HEAD_DIM), bf16),
                pltpu.VMEM((QBLOCK // n_head, KV_HEADS * HEAD_DIM), bf16),
                pltpu.VMEM((GROUP * QBLOCK, HEAD_DIM), bf16),
                pltpu.VMEM((GROUP * QBLOCK, HEAD_DIM), bf16),
                pltpu.VMEM((GROUP, QBLOCK), f32),
                pltpu.VMEM((GROUP, QBLOCK), f32),
                pltpu.VMEM((n_tok, QBLOCK), jnp.int32),
                pltpu.SMEM((n_tok,), jnp.int32),
                pltpu.VMEM((slots, QBLOCK, HEAD_DIM), bf16),
                pltpu.VMEM((slots, QBLOCK, HEAD_DIM), bf16),
                pltpu.VMEM((HEAD_DIM, slots * QBLOCK), bf16),
                pltpu.VMEM((slots, QBLOCK, GROUP * QBLOCK), bf16),
                pltpu.VMEM((REACH, 2, QBLOCK, HEAD_DIM), bf16),
                pltpu.VMEM((REACH, 2, QBLOCK, HEAD_DIM), bf16),
                pltpu.VMEM((REACH, 2, QBLOCK, HEAD_DIM), bf16),
                pltpu.VMEM((slots, 2, QBLOCK, HEAD_DIM), f32),
                pltpu.SemaphoreType.DMA((2,)),
                pltpu.SemaphoreType.DMA((2 * GROUP + 4,)),
                pltpu.SemaphoreType.DMA((2, n_head - 1)),
                pltpu.SemaphoreType.DMA((2, PIECES)),
                pltpu.SemaphoreType.DMA((REACH, 2, PIECES)),
                pltpu.SemaphoreType.DMA((REACH, 2, PIECES)),
                pltpu.SemaphoreType.DMA((REACH,)),
                pltpu.SemaphoreType.DMA((REACH,)),
                pltpu.SemaphoreType.DMA((REACH,)),
                pltpu.SemaphoreType.DMA((2, n_head)),
                pltpu.SemaphoreType.REGULAR,
            ],
            compiler_params=pltpu.CompilerParams(
                collective_id=0, has_side_effects=True
            ),
        )(query, keys, values, out_grad, log_norm, row_dot, starts, spans)
        return pl.pallas_call(
            store,
            out_shape=shapes,
            in_specs=[inside] * 3,
            out_specs=(anywhere,) * 3,
            scratch_shapes=[pltpu.SemaphoreType.DMA((3,))],
            compiler_params=pltpu.CompilerParams(vmem_limit_bytes=4 << 20),
        )(*grads)

    return jax.shard_map(
        per_device,
        mesh=mesh,
        in_specs=(
            P("tok", "head"),
            P(("tok", "head"), None),
            P(("tok", "head"), None),
            P("tok", "head"),
            P("head", "tok"),
            P("head", "tok"),
            P(),
            P(),
        ),
        out_specs=(P("tok", "head"), P("tok", "head"), P("tok", "head")),
        check_vma=False,
    )
```

```python
import functools
import math

import jax
import jax.numpy as jnp
from jax import lax
from jax.experimental import pallas as pl
from jax.experimental.pallas import tpu as pltpu
from jax.sharding import PartitionSpec as P

HEADS = 64
KV_HEADS = 8
HEAD_DIM = 128
QBLOCK = 128
REACH = 5
GROUP = HEADS // KV_HEADS
PIECES = 4
MESH = pl.DeviceIdType.MESH
FAR = 1 << 30
NS = jax.named_scope
JOIN = 3
ROW = 32

NT = (((1,), (1,)), ((), ()))
NN = (((1,), (0,)), ((), ()))


def matmul(a, b, dims):
    return lax.dot_general(a, b, dims, preferred_element_type=jnp.float32)


def kernel(
    n_tok,
    n_head,
    query_hbm,
    keys_hbm,
    values_hbm,
    outgrad_hbm,
    norm_hbm,
    dot_hbm,
    starts_hbm,
    spans_hbm,
    dq_out,
    dk_out,
    dv_out,
    stage_s,
    rows_s,
    norms_s,
    starts_s,
    spans_s,
    key_win,
    value_win,
    key_t,
    ds_all,
    probs_s,
    send_buf,
    recv_buf,
    join_buf,
    terms,
    stage_sem,
    in_sem,
    a2a_send,
    own_sem,
    kv_send,
    kv_recv,
    grad_send,
    grad_recv,
    join_recv,
    next_send,
    turn,
):
    scale = 1.0 / math.sqrt(HEAD_DIM)
    tok = lax.axis_index("tok")
    head = lax.axis_index("head")
    rows = QBLOCK // n_head
    half = QBLOCK // PIECES

    place = lax.rem(tok, ROW)

    def tok_at(step):
        return lax.rem(tok + (step + n_tok), n_tok)

    slot_rows = pl.ds(pl.multiple_of(head * rows, rows), rows)
    my_half = lax.div(head, n_head // PIECES)

    def columns(h):
        return pl.ds(pl.multiple_of(h * HEAD_DIM, HEAD_DIM), HEAD_DIM)

    barrier = pltpu.get_barrier_semaphore()
    with NS("xsig"):
        for step in range(1, n_head):
            pl.semaphore_signal(
                barrier, 1, device_id={"head": lax.rem(head + step, n_head)}, device_id_type=MESH
            )

        @pl.when(tok > 0)
        def _():
            for step in range(n_head):
                pl.semaphore_signal(
                    barrier,
                    1,
                    device_id={"tok": tok_at(-1), "head": lax.rem(head + step, n_head)},
                    device_id_type=MESH,
                )

    sides = ((keys_hbm, stage_s.at[0], key_win), (values_hbm, stage_s.at[1], value_win))
    q_s, do_s = rows_s.at[0], rows_s.at[1]
    norm_s, dot_s = norms_s.at[0], norms_s.at[1]
    with NS("xld"):
        for side, (source, stage, window) in enumerate(sides):
            pltpu.make_async_copy(
                source.at[:, columns(head)], window.at[0, slot_rows, :], own_sem.at[side]
            ).start()
            pltpu.make_async_copy(source, stage, stage_sem).start()
        for h in range(GROUP):
            block = pl.ds(h * QBLOCK, QBLOCK)
            cols = pl.ds(h * HEAD_DIM, HEAD_DIM)
            pltpu.make_async_copy(query_hbm.at[:, cols], q_s.at[block, :], in_sem.at[0]).start()
            pltpu.make_async_copy(outgrad_hbm.at[:, cols], do_s.at[block, :], in_sem.at[0]).start()
        pltpu.make_async_copy(norm_hbm, norm_s, in_sem.at[1]).start()
        pltpu.make_async_copy(dot_hbm, dot_s, in_sem.at[1]).start()
        pltpu.make_async_copy(starts_hbm, starts_s, in_sem.at[2]).start()
        pltpu.make_async_copy(spans_hbm, spans_s, in_sem.at[3]).start()

    def finished(view, sem):
        pltpu.make_async_copy(view, view, sem).wait()

    with NS("xstage"):
        finished(stage_s, stage_sem)
    with NS("xbar"):
        waits = n_head - 1 + jnp.where(tok + 1 < n_tok, n_head, 0)
        pl.semaphore_wait(barrier, waits)

    def to_next(side, step):
        _, stage, window = sides[side]
        peer = lax.rem(head + step, n_head)
        return pltpu.make_async_remote_copy(
            src_ref=stage.at[:, columns(peer)],
            dst_ref=window.at[1, slot_rows, :],
            send_sem=next_send,
            recv_sem=kv_recv.at[side * PIECES + my_half],
            device_id={"tok": tok_at(1), "head": peer},
            device_id_type=MESH,
        )

    with NS("xspread"):
        for side, (_, stage, window) in enumerate(sides):

            @pl.when(tok + 1 < n_tok)
            def _():
                for step in range(n_head):
                    to_next(side, step).start()

        for side, (_, stage, window) in enumerate(sides):
            for step in range(1, n_head):
                peer = lax.rem(head + step, n_head)
                pltpu.make_async_remote_copy(
                    src_ref=stage.at[:, columns(peer)],
                    dst_ref=window.at[0, slot_rows, :],
                    send_sem=a2a_send,
                    recv_sem=own_sem.at[side],
                    device_id={"head": peer},
                    device_id_type=MESH,
                ).start()

    def piece(slot, side, part):
        window = (key_win, value_win)[side]
        return window.at[slot, pl.ds(part * half, half), :]

    def arrival(slot, side, part):
        index = (slot - 1) * 2 * PIECES
        return kv_recv.at[index + (side if slot == REACH else side * PIECES + part)]

    def forward(slot, side, part):
        return pltpu.make_async_remote_copy(
            src_ref=piece(slot, side, part),
            dst_ref=piece(slot + 1, side, part),
            send_sem=kv_send.at[slot - 1],
            recv_sem=arrival(slot + 1, side, part),
            device_id={"tok": tok_at(1)},
            device_id_type=MESH,
        )

    def forwards(slot):
        return (tok >= slot) & (tok + 1 < n_tok)

    pieces = [(side, part) for side in range(2) for part in range(PIECES)]
    with NS("xa2a"):
        for side in range(2):
            finished(sides[side][2].at[0], own_sem.at[side])
    with NS("xloads"):
        finished(rows_s, in_sem.at[0])
        finished(norms_s, in_sem.at[1])
        finished(starts_s, in_sem.at[2])
        finished(spans_s, in_sem.at[3])

    start_row = starts_s[pl.ds(tok, 1), :]
    span = spans_s[tok]
    row_iota = lax.broadcasted_iota(jnp.int32, (QBLOCK, QBLOCK), 0)
    col_iota = lax.broadcasted_iota(jnp.int32, (QBLOCK, QBLOCK), 1)

    def mask(slot):
        key_pos = row_iota + (tok - slot) * QBLOCK
        allowed = key_pos >= jnp.where(slot < span, start_row, FAR)
        if slot == 0:
            allowed = allowed & (row_iota <= col_iota)
        return allowed

    def pair_probs(key, pair, allowed):
        scores = matmul(key, q_s[pl.ds(pair * 2 * QBLOCK, 2 * QBLOCK), :], NT)
        probs = []
        for e in range(2):
            part = scores[:, e * QBLOCK : (e + 1) * QBLOCK] * scale
            part = jnp.exp(part - norm_s[pl.ds(pair * 2 + e, 1), :])
            probs.append(jnp.where(allowed, part, 0.0))
        return probs

    def pair_grads(value, pair, probs):
        prob_grad = matmul(value, do_s[pl.ds(pair * 2 * QBLOCK, 2 * QBLOCK), :], NT)
        grads = []
        for e in range(2):
            part = prob_grad[:, e * QBLOCK : (e + 1) * QBLOCK]
            part = probs[e] * (part - dot_s[pl.ds(pair * 2 + e, 1), :])
            grads.append(part.astype(jnp.bfloat16))
        return jnp.concatenate(grads, axis=1)

    def lowered(probs):
        return jnp.concatenate([part.astype(jnp.bfloat16) for part in probs], axis=1)

    def block(slot):
        key = key_win[slot]
        value = value_win[slot]
        allowed = mask(slot)
        value_term = jnp.zeros((QBLOCK, HEAD_DIM), jnp.float32)
        key_term = jnp.zeros((QBLOCK, HEAD_DIM), jnp.float32)
        for pair in range(GROUP // 2):
            rows_of = pl.ds(pair * 2 * QBLOCK, 2 * QBLOCK)
            probs = pair_probs(key, pair, allowed)
            grad = pair_grads(value, pair, probs)
            ds_all[slot, :, rows_of] = grad
            value_term = value_term + matmul(lowered(probs), do_s[rows_of, :], NN)
            key_term = key_term + matmul(grad, q_s[rows_of, :], NN)
        key_t[:, pl.ds(slot * QBLOCK, QBLOCK)] = key.T
        return key_term * scale, value_term

    def value_half(slot):
        key = key_win[slot]
        allowed = mask(slot)
        value_term = jnp.zeros((QBLOCK, HEAD_DIM), jnp.float32)
        for pair in range(GROUP // 2):
            rows_of = pl.ds(pair * 2 * QBLOCK, 2 * QBLOCK)
            probs = pair_probs(key, pair, allowed)
            for e in range(2):
                probs_s[:, pl.ds((pair * 2 + e) * QBLOCK, QBLOCK)] = probs[e]
            value_term = value_term + matmul(lowered(probs), do_s[rows_of, :], NN)
        key_t[:, pl.ds(slot * QBLOCK, QBLOCK)] = key.T
        terms[slot, 1] = value_term

    def key_half(slot):
        value = value_win[slot]
        key_term = jnp.zeros((QBLOCK, HEAD_DIM), jnp.float32)
        for pair in range(GROUP // 2):
            rows_of = pl.ds(pair * 2 * QBLOCK, 2 * QBLOCK)
            probs = [probs_s[:, pl.ds((pair * 2 + e) * QBLOCK, QBLOCK)] for e in range(2)]
            grad = pair_grads(value, pair, probs)
            ds_all[slot, :, rows_of] = grad
            key_term = key_term + matmul(grad, q_s[rows_of, :], NN)
        terms[slot, 0] = key_term * scale

    def home(slot):
        return pltpu.make_async_remote_copy(
            src_ref=send_buf.at[slot - 1],
            dst_ref=recv_buf.at[slot - 1],
            send_sem=grad_send.at[slot - 1],
            recv_sem=grad_recv.at[slot - 1],
            device_id={"tok": tok_at(-slot)},
            device_id_type=MESH,
        )

    def onward(slot):
        return pltpu.make_async_remote_copy(
            src_ref=send_buf.at[slot - 1],
            dst_ref=join_buf.at[slot - 1],
            send_sem=grad_send.at[slot - 1],
            recv_sem=join_recv.at[slot - JOIN],
            device_id={"tok": tok_at(1)},
            device_id_type=MESH,
        )

    def goes_on(slot):
        if slot < JOIN or slot == REACH:
            return False
        return place != ROW - 1

    def joins(slot):
        if slot <= JOIN:
            return False
        return (place != 0) & (tok >= slot)

    def compute(slot):
        with NS(f"xblock{slot}"):
            both = block(slot)
            for side in range(2):
                terms[slot, side] = both[side]

    def ship(slot):
        with NS(f"xship{slot}"):
            if joins(slot) is False:
                for side in range(2):
                    send_buf[slot - 1, side] = terms[slot, side].astype(jnp.bfloat16)
            else:

                @pl.when(joins(slot))
                def _():
                    onward(slot - 1).wait_recv()
                    for side in range(2):
                        send_buf[slot - 1, side] = (
                            terms[slot, side] + join_buf[slot - 2, side].astype(jnp.float32)
                        ).astype(jnp.bfloat16)

                @pl.when(jnp.logical_not(joins(slot)))
                def _():
                    for side in range(2):
                        send_buf[slot - 1, side] = terms[slot, side].astype(jnp.bfloat16)

            passing = goes_on(slot)
            if passing is False:
                home(slot).start()
            else:

                @pl.when(passing)
                def _():
                    onward(slot).start()

                @pl.when(jnp.logical_not(passing))
                def _():
                    home(slot).start()

    def home_side(side):
        return pltpu.make_async_remote_copy(
            src_ref=send_buf.at[REACH - 1, side],
            dst_ref=recv_buf.at[REACH - 1, side],
            send_sem=grad_send.at[REACH - 1],
            recv_sem=grad_recv.at[REACH - 1],
            device_id={"tok": tok_at(-REACH)},
            device_id_type=MESH,
        )

    early = (place == 0) & (tok >= REACH)

    def early_side(side):
        @pl.when(early)
        def _():
            send_buf[REACH - 1, side] = terms[REACH, side].astype(jnp.bfloat16)
            home_side(side).start()

    def arrive(slot):
        for side, part in pieces:
            with NS(f"xkv{slot}{side}{part}"):
                finished(piece(slot, side, part), arrival(slot, side, part))

            @pl.when(forwards(slot))
            def _():
                forward(slot, side, part).start()

    def last():
        with NS("xkv500"):
            finished(key_win.at[REACH], arrival(REACH, 0, 0))
        with NS("xhalf"):
            value_half(REACH)
        early_side(1)
        with NS("xkv510"):
            finished(value_win.at[REACH], arrival(REACH, 1, 0))
        with NS("xblock5"):
            key_half(REACH)
        early_side(0)

    compute(0)
    for slot in range(1, REACH + 1):

        @pl.when(tok >= slot)
        def _():
            if slot == REACH:
                last()
            else:
                arrive(slot)
                compute(slot)
                ship(slot)

        @pl.when(tok < slot)
        def _():
            ds_all[slot] = jnp.zeros((QBLOCK, GROUP * QBLOCK), jnp.bfloat16)
            key_t[:, pl.ds(slot * QBLOCK, QBLOCK)] = jnp.zeros((HEAD_DIM, QBLOCK), jnp.bfloat16)

    crossing = (place < REACH) & (tok >= ROW)

    def pass_turn():
        @pl.when(crossing & (place < REACH - 1))
        def _():
            pl.semaphore_signal(turn, 1, device_id={"tok": tok_at(1)}, device_id_type=MESH)

    @pl.when(early)
    def _():
        pass_turn()

    with NS("xdq"):
        for pair in range(GROUP // 2):
            lanes = pl.ds(pair * 2 * QBLOCK, 2 * QBLOCK)
            grad = ds_all[:, :, lanes].reshape((REACH + 1) * QBLOCK, 2 * QBLOCK)
            dq_t = matmul(key_t[...], grad, NN) * scale
            for e in range(2):
                h = pair * 2 + e
                dq_out[:, pl.ds(h * HEAD_DIM, HEAD_DIM)] = (
                    dq_t[:, e * QBLOCK : (e + 1) * QBLOCK].T.astype(jnp.bfloat16)
                )

    @pl.when((tok >= REACH) & jnp.logical_not(early))
    def _():
        @pl.when(crossing)
        def _():
            pl.semaphore_wait(turn, 1)

        ship(REACH)
        pass_turn()

    for slot in range(1, REACH + 1):
        expected = tok + slot < n_tok
        if JOIN <= slot < REACH:
            expected = place + slot == ROW - 1
        with NS(f"xgrad{slot}"):

            @pl.when(expected)
            def _():
                home(slot).wait_recv()
                for side in range(2):
                    terms[0, side] += recv_buf[slot - 1, side].astype(jnp.float32)

    for side, out in enumerate((dk_out, dv_out)):
        out[...] = terms[0, side].astype(jnp.bfloat16)
    with NS("xsends"):
        finished(q_s.at[pl.ds(0, 2 * (n_head - 1) * rows), :], a2a_send)

        @pl.when(tok + 1 < n_tok)
        def _():
            finished(q_s.at[pl.ds(0, 2 * n_head * rows), :], next_send)

        for slot in range(1, REACH):

            @pl.when(forwards(slot))
            def _():
                finished(q_s.at[pl.ds(0, 2 * QBLOCK), :], kv_send.at[slot - 1])

    with NS("xsendg"):
        for slot in range(1, REACH + 1):

            @pl.when(tok >= slot)
            def _():
                home(slot).wait_send()


def store(dq_ref, dk_ref, dv_ref, dq_hbm, dk_hbm, dv_hbm, sems):
    copies = [
        pltpu.make_async_copy(source, target, sems.at[index])
        for index, (source, target) in enumerate(
            ((dq_ref, dq_hbm), (dk_ref, dk_hbm), (dv_ref, dv_hbm))
        )
    ]
    for copy in copies:
        copy.start()
    for copy in copies:
        copy.wait()


def solution(mesh):
    n_tok = mesh.shape["tok"]
    n_head = mesh.shape["head"]
    slots = REACH + 1
    bf16, f32 = jnp.bfloat16, jnp.float32

    def per_device(query, keys, values, out_grad, log_norm, row_dot, doc_start, spans):
        starts = doc_start.reshape(n_tok, QBLOCK)
        anywhere = pl.BlockSpec(memory_space=pl.ANY)
        outside = pl.BlockSpec(memory_space=pltpu.HBM)
        inside = pl.BlockSpec(memory_space=pltpu.VMEM)
        shapes = (
            jax.ShapeDtypeStruct((QBLOCK, GROUP * HEAD_DIM), bf16),
            jax.ShapeDtypeStruct((QBLOCK, HEAD_DIM), bf16),
            jax.ShapeDtypeStruct((QBLOCK, HEAD_DIM), bf16),
        )
        grads = pl.pallas_call(
            functools.partial(kernel, n_tok, n_head),
            out_shape=tuple(pltpu.VMEM(shape.shape, shape.dtype) for shape in shapes),
            in_specs=[outside] * 8,
            out_specs=(inside,) * 3,
            scratch_shapes=[
                pltpu.VMEM((2, QBLOCK // n_head, KV_HEADS * HEAD_DIM), bf16),
                pltpu.VMEM((2, GROUP * QBLOCK, HEAD_DIM), bf16),
                pltpu.VMEM((2, GROUP, QBLOCK), f32),
                pltpu.VMEM((n_tok, QBLOCK), jnp.int32),
                pltpu.SMEM((n_tok,), jnp.int32),
                pltpu.VMEM((slots, QBLOCK, HEAD_DIM), bf16),
                pltpu.VMEM((slots, QBLOCK, HEAD_DIM), bf16),
                pltpu.VMEM((HEAD_DIM, slots * QBLOCK), bf16),
                pltpu.VMEM((slots, QBLOCK, GROUP * QBLOCK), bf16),
                pltpu.VMEM((QBLOCK, GROUP * QBLOCK), f32),
                pltpu.VMEM((REACH, 2, QBLOCK, HEAD_DIM), bf16),
                pltpu.VMEM((REACH, 2, QBLOCK, HEAD_DIM), bf16),
                pltpu.VMEM((REACH, 2, QBLOCK, HEAD_DIM), bf16),
                pltpu.VMEM((slots, 2, QBLOCK, HEAD_DIM), f32),
                pltpu.SemaphoreType.DMA(()),
                pltpu.SemaphoreType.DMA((4,)),
                pltpu.SemaphoreType.DMA(()),
                pltpu.SemaphoreType.DMA((2,)),
                pltpu.SemaphoreType.DMA((REACH - 1,)),
                pltpu.SemaphoreType.DMA(((REACH - 1) * 2 * PIECES + 2,)),
                pltpu.SemaphoreType.DMA((REACH,)),
                pltpu.SemaphoreType.DMA((REACH,)),
                pltpu.SemaphoreType.DMA((REACH - JOIN,)),
                pltpu.SemaphoreType.DMA(()),
                pltpu.SemaphoreType.REGULAR,
            ],
            compiler_params=pltpu.CompilerParams(
                collective_id=0, has_side_effects=True
            ),
        )(query, keys, values, out_grad, log_norm, row_dot, starts, spans)
        return pl.pallas_call(
            store,
            out_shape=shapes,
            in_specs=[inside] * 3,
            out_specs=(anywhere,) * 3,
            scratch_shapes=[pltpu.SemaphoreType.DMA((3,))],
            compiler_params=pltpu.CompilerParams(vmem_limit_bytes=4 << 20),
        )(*grads)

    return jax.shard_map(
        per_device,
        mesh=mesh,
        in_specs=(
            P("tok", "head"),
            P(("tok", "head"), None),
            P(("tok", "head"), None),
            P("tok", "head"),
            P("head", "tok"),
            P("head", "tok"),
            P(),
            P(),
        ),
        out_specs=(P("tok", "head"), P("tok", "head"), P("tok", "head")),
        check_vma=False,
    )
```

```python
import functools
import math

import jax
import jax.numpy as jnp
from jax import lax
from jax.experimental import pallas as pl
from jax.experimental.pallas import tpu as pltpu
from jax.sharding import PartitionSpec as P

HEADS = 64
KV_HEADS = 8
HEAD_DIM = 128
QBLOCK = 128
REACH = 5
GROUP = HEADS // KV_HEADS
PIECES = 4
STRIPS = 4
MESH = pl.DeviceIdType.MESH
FAR = 1 << 30
NS = jax.named_scope
JOIN = 4
ROW = 32

NT = (((1,), (1,)), ((), ()))
NN = (((1,), (0,)), ((), ()))


def matmul(a, b, dims):
    return lax.dot_general(a, b, dims, preferred_element_type=jnp.float32)


def kernel(
    n_tok,
    n_head,
    query_hbm,
    keys_hbm,
    values_hbm,
    outgrad_hbm,
    norm_hbm,
    dot_hbm,
    starts_hbm,
    spans_hbm,
    dq_out,
    dk_out,
    dv_out,
    stage_s,
    rows_s,
    norms_s,
    starts_s,
    spans_s,
    key_win,
    value_win,
    key_t,
    ds_all,
    probs_s,
    send_buf,
    recv_buf,
    join_buf,
    terms,
    stage_sem,
    in_sem,
    a2a_send,
    own_sem,
    kv_send,
    kv_recv,
    grad_send,
    grad_recv,
    join_recv,
    next_send,
    turn,
):
    scale = 1.0 / math.sqrt(HEAD_DIM)
    tok = lax.axis_index("tok")
    head = lax.axis_index("head")
    rows = QBLOCK // n_head
    half = QBLOCK // PIECES

    place = lax.rem(tok, ROW)

    def tok_at(step):
        return lax.rem(tok + (step + n_tok), n_tok)

    slot_rows = pl.ds(pl.multiple_of(head * rows, rows), rows)
    my_half = lax.div(head, n_head // PIECES)

    def columns(h):
        return pl.ds(pl.multiple_of(h * HEAD_DIM, HEAD_DIM), HEAD_DIM)

    barrier = pltpu.get_barrier_semaphore()
    with NS("xsig"):
        for step in range(1, n_head):
            pl.semaphore_signal(
                barrier, 1, device_id={"head": lax.rem(head + step, n_head)}, device_id_type=MESH
            )

        @pl.when(tok > 0)
        def _():
            for step in range(n_head):
                pl.semaphore_signal(
                    barrier,
                    1,
                    device_id={"tok": tok_at(-1), "head": lax.rem(head + step, n_head)},
                    device_id_type=MESH,
                )

    sides = ((keys_hbm, stage_s.at[0], key_win), (values_hbm, stage_s.at[1], value_win))
    q_s, do_s = rows_s.at[0], rows_s.at[1]
    norm_s, dot_s = norms_s.at[0], norms_s.at[1]
    with NS("xld"):
        for side, (source, stage, window) in enumerate(sides):
            pltpu.make_async_copy(
                source.at[:, columns(head)], window.at[0, slot_rows, :], own_sem.at[side]
            ).start()
            pltpu.make_async_copy(source, stage, stage_sem).start()
        for h in range(GROUP):
            block = pl.ds(h * QBLOCK, QBLOCK)
            cols = pl.ds(h * HEAD_DIM, HEAD_DIM)
            pltpu.make_async_copy(query_hbm.at[:, cols], q_s.at[block, :], in_sem.at[0]).start()
            pltpu.make_async_copy(outgrad_hbm.at[:, cols], do_s.at[block, :], in_sem.at[0]).start()
        pltpu.make_async_copy(norm_hbm, norm_s, in_sem.at[1]).start()
        pltpu.make_async_copy(dot_hbm, dot_s, in_sem.at[1]).start()
        pltpu.make_async_copy(starts_hbm, starts_s, in_sem.at[2]).start()
        pltpu.make_async_copy(spans_hbm, spans_s, in_sem.at[3]).start()

    def finished(view, sem):
        pltpu.make_async_copy(view, view, sem).wait()

    with NS("xstage"):
        finished(stage_s, stage_sem)
    with NS("xbar"):
        waits = n_head - 1 + jnp.where(tok + 1 < n_tok, n_head, 0)
        pl.semaphore_wait(barrier, waits)

    def to_next(side, step):
        _, stage, window = sides[side]
        peer = lax.rem(head + step, n_head)
        return pltpu.make_async_remote_copy(
            src_ref=stage.at[:, columns(peer)],
            dst_ref=window.at[1, slot_rows, :],
            send_sem=next_send,
            recv_sem=kv_recv.at[side * PIECES + my_half],
            device_id={"tok": tok_at(1), "head": peer},
            device_id_type=MESH,
        )

    with NS("xspread"):
        for side, (_, stage, window) in enumerate(sides):

            @pl.when(tok + 1 < n_tok)
            def _():
                for step in range(n_head):
                    to_next(side, step).start()

        for side, (_, stage, window) in enumerate(sides):
            for step in range(1, n_head):
                peer = lax.rem(head + step, n_head)
                pltpu.make_async_remote_copy(
                    src_ref=stage.at[:, columns(peer)],
                    dst_ref=window.at[0, slot_rows, :],
                    send_sem=a2a_send,
                    recv_sem=own_sem.at[side],
                    device_id={"head": peer},
                    device_id_type=MESH,
                ).start()

    def piece(slot, side, part):
        window = (key_win, value_win)[side]
        return window.at[slot, pl.ds(part * half, half), :]

    def arrival(slot, side, part):
        index = (slot - 1) * 2 * PIECES
        return kv_recv.at[index + (side if slot == REACH else side * PIECES + part)]

    def forward(slot, side, part):
        return pltpu.make_async_remote_copy(
            src_ref=piece(slot, side, part),
            dst_ref=piece(slot + 1, side, part),
            send_sem=kv_send.at[slot - 1],
            recv_sem=arrival(slot + 1, side, part),
            device_id={"tok": tok_at(1)},
            device_id_type=MESH,
        )

    def forwards(slot):
        return (tok >= slot) & (tok + 1 < n_tok)

    pieces = [(side, part) for side in range(2) for part in range(PIECES)]
    with NS("xa2a"):
        for side in range(2):
            finished(sides[side][2].at[0], own_sem.at[side])
    with NS("xloads"):
        finished(rows_s, in_sem.at[0])
        finished(norms_s, in_sem.at[1])
        finished(starts_s, in_sem.at[2])
        finished(spans_s, in_sem.at[3])

    start_row = starts_s[pl.ds(tok, 1), :]
    span = spans_s[tok]
    row_iota = lax.broadcasted_iota(jnp.int32, (QBLOCK, QBLOCK), 0)
    col_iota = lax.broadcasted_iota(jnp.int32, (QBLOCK, QBLOCK), 1)

    def mask(slot):
        key_pos = row_iota + (tok - slot) * QBLOCK
        allowed = key_pos >= jnp.where(slot < span, start_row, FAR)
        if slot == 0:
            allowed = allowed & (row_iota <= col_iota)
        return allowed

    def pair_probs(key, pair, allowed):
        scores = matmul(key, q_s[pl.ds(pair * 2 * QBLOCK, 2 * QBLOCK), :], NT)
        probs = []
        for e in range(2):
            part = scores[:, e * QBLOCK : (e + 1) * QBLOCK] * scale
            part = jnp.exp(part - norm_s[pl.ds(pair * 2 + e, 1), :])
            probs.append(jnp.where(allowed, part, 0.0))
        return probs

    def pair_grads(value, pair, probs):
        prob_grad = matmul(value, do_s[pl.ds(pair * 2 * QBLOCK, 2 * QBLOCK), :], NT)
        grads = []
        for e in range(2):
            part = prob_grad[:, e * QBLOCK : (e + 1) * QBLOCK]
            part = probs[e] * (part - dot_s[pl.ds(pair * 2 + e, 1), :])
            grads.append(part.astype(jnp.bfloat16))
        return jnp.concatenate(grads, axis=1)

    def lowered(probs):
        return jnp.concatenate([part.astype(jnp.bfloat16) for part in probs], axis=1)

    def block(slot):
        key = key_win[slot]
        value = value_win[slot]
        allowed = mask(slot)
        value_term = jnp.zeros((QBLOCK, HEAD_DIM), jnp.float32)
        key_term = jnp.zeros((QBLOCK, HEAD_DIM), jnp.float32)
        for pair in range(GROUP // 2):
            rows_of = pl.ds(pair * 2 * QBLOCK, 2 * QBLOCK)
            probs = pair_probs(key, pair, allowed)
            grad = pair_grads(value, pair, probs)
            ds_all[slot, :, rows_of] = grad
            value_term = value_term + matmul(lowered(probs), do_s[rows_of, :], NN)
            key_term = key_term + matmul(grad, q_s[rows_of, :], NN)
        key_t[:, pl.ds(slot * QBLOCK, QBLOCK)] = key.T
        return key_term * scale, value_term

    def value_half(slot):
        key = key_win[slot]
        allowed = mask(slot)
        value_term = jnp.zeros((QBLOCK, HEAD_DIM), jnp.float32)
        for pair in range(GROUP // 2):
            rows_of = pl.ds(pair * 2 * QBLOCK, 2 * QBLOCK)
            probs = pair_probs(key, pair, allowed)
            for e in range(2):
                probs_s[:, pl.ds((pair * 2 + e) * QBLOCK, QBLOCK)] = probs[e]
            value_term = value_term + matmul(lowered(probs), do_s[rows_of, :], NN)
        key_t[:, pl.ds(slot * QBLOCK, QBLOCK)] = key.T
        terms[slot, 1] = value_term

    def key_half(slot):
        value = value_win[slot]
        key_term = jnp.zeros((QBLOCK, HEAD_DIM), jnp.float32)
        for pair in range(GROUP // 2):
            rows_of = pl.ds(pair * 2 * QBLOCK, 2 * QBLOCK)
            probs = [probs_s[:, pl.ds((pair * 2 + e) * QBLOCK, QBLOCK)] for e in range(2)]
            grad = pair_grads(value, pair, probs)
            ds_all[slot, :, rows_of] = grad
            key_term = key_term + matmul(grad, q_s[rows_of, :], NN)
        terms[slot, 0] = key_term * scale

    def home(slot):
        return pltpu.make_async_remote_copy(
            src_ref=send_buf.at[slot - 1],
            dst_ref=recv_buf.at[slot - 1],
            send_sem=grad_send.at[slot - 1],
            recv_sem=grad_recv.at[slot - 1],
            device_id={"tok": tok_at(-slot)},
            device_id_type=MESH,
        )

    def onward(slot):
        return pltpu.make_async_remote_copy(
            src_ref=send_buf.at[slot - 1],
            dst_ref=join_buf.at[slot - 1],
            send_sem=grad_send.at[slot - 1],
            recv_sem=join_recv.at[slot - JOIN],
            device_id={"tok": tok_at(1)},
            device_id_type=MESH,
        )

    def goes_on(slot):
        if slot < JOIN or slot == REACH:
            return False
        return place != ROW - 1

    def joins(slot):
        if slot <= JOIN:
            return False
        return (place != 0) & (tok >= slot)

    def compute(slot):
        with NS(f"xblock{slot}"):
            both = block(slot)
            for side in range(2):
                terms[slot, side] = both[side]

    def ship(slot):
        with NS(f"xship{slot}"):
            if joins(slot) is False:
                for side in range(2):
                    send_buf[slot - 1, side] = terms[slot, side].astype(jnp.bfloat16)
            else:

                @pl.when(joins(slot))
                def _():
                    onward(slot - 1).wait_recv()
                    for side in range(2):
                        send_buf[slot - 1, side] = (
                            terms[slot, side] + join_buf[slot - 2, side].astype(jnp.float32)
                        ).astype(jnp.bfloat16)

                @pl.when(jnp.logical_not(joins(slot)))
                def _():
                    for side in range(2):
                        send_buf[slot - 1, side] = terms[slot, side].astype(jnp.bfloat16)

            passing = goes_on(slot)
            if passing is False:
                home(slot).start()
            else:

                @pl.when(passing)
                def _():
                    onward(slot).start()

                @pl.when(jnp.logical_not(passing))
                def _():
                    home(slot).start()

    def home_side(side):
        return pltpu.make_async_remote_copy(
            src_ref=send_buf.at[REACH - 1, side],
            dst_ref=recv_buf.at[REACH - 1, side],
            send_sem=grad_send.at[REACH - 1],
            recv_sem=grad_recv.at[REACH - 1],
            device_id={"tok": tok_at(-REACH)},
            device_id_type=MESH,
        )

    early = (place == 0) & (tok >= REACH)

    crossing = (place < REACH) & (tok >= ROW)

    def pass_turn():
        @pl.when(crossing & (place < REACH - 1))
        def _():
            pl.semaphore_signal(turn, 1, device_id={"tok": tok_at(1)}, device_id_type=MESH)

    def early_side(side):
        @pl.when(early)
        def _():
            send_buf[REACH - 1, side] = terms[REACH, side].astype(jnp.bfloat16)
            home_side(side).start()
            if side == 1:
                pass_turn()

    def arrive(slot):
        for side, part in pieces:
            with NS(f"xkv{slot}{side}{part}"):
                finished(piece(slot, side, part), arrival(slot, side, part))

            @pl.when(forwards(slot))
            def _():
                forward(slot, side, part).start()

    def last():
        with NS("xkv500"):
            finished(key_win.at[REACH], arrival(REACH, 0, 0))
        with NS("xhalf"):
            value_half(REACH)
        early_side(1)
        with NS("xkv510"):
            finished(value_win.at[REACH], arrival(REACH, 1, 0))
        with NS("xblock5"):
            key_half(REACH)
        early_side(0)

    compute(0)
    for slot in range(1, REACH + 1):

        @pl.when(tok >= slot)
        def _():
            if slot == REACH:
                last()
            else:
                arrive(slot)
                compute(slot)
                ship(slot)

        @pl.when(tok < slot)
        def _():
            ds_all[slot] = jnp.zeros((QBLOCK, GROUP * QBLOCK), jnp.bfloat16)
            key_t[:, pl.ds(slot * QBLOCK, QBLOCK)] = jnp.zeros((HEAD_DIM, QBLOCK), jnp.bfloat16)

    with NS("xdq"):
        for pair in range(GROUP // 2):
            lanes = pl.ds(pair * 2 * QBLOCK, 2 * QBLOCK)
            grad = ds_all[:, :, lanes].reshape((REACH + 1) * QBLOCK, 2 * QBLOCK)
            dq_t = matmul(key_t[...], grad, NN) * scale
            for e in range(2):
                h = pair * 2 + e
                dq_out[:, pl.ds(h * HEAD_DIM, HEAD_DIM)] = (
                    dq_t[:, e * QBLOCK : (e + 1) * QBLOCK].T.astype(jnp.bfloat16)
                )

    @pl.when((tok >= REACH) & jnp.logical_not(early))
    def _():
        @pl.when(crossing)
        def _():
            pl.semaphore_wait(turn, 1)

        ship(REACH)
        pass_turn()

    for slot in range(1, REACH + 1):
        expected = tok + slot < n_tok
        if JOIN <= slot < REACH:
            expected = place + slot == ROW - 1
        with NS(f"xgrad{slot}"):

            @pl.when(expected)
            def _():
                home(slot).wait_recv()
                for side in range(2):
                    terms[0, side] += recv_buf[slot - 1, side].astype(jnp.float32)

    for side, out in enumerate((dk_out, dv_out)):
        out[...] = terms[0, side].astype(jnp.bfloat16)
    with NS("xsends"):
        finished(q_s.at[pl.ds(0, 2 * (n_head - 1) * rows), :], a2a_send)

        @pl.when(tok + 1 < n_tok)
        def _():
            finished(q_s.at[pl.ds(0, 2 * n_head * rows), :], next_send)

        for slot in range(1, REACH):

            @pl.when(forwards(slot))
            def _():
                finished(q_s.at[pl.ds(0, 2 * QBLOCK), :], kv_send.at[slot - 1])

    with NS("xsendg"):
        for slot in range(1, REACH + 1):

            @pl.when(tok >= slot)
            def _():
                home(slot).wait_send()


def store(dq_ref, dk_ref, dv_ref, dq_hbm, dk_hbm, dv_hbm, sems):
    part = QBLOCK // STRIPS
    moves = [
        (dq_ref.at[pl.ds(strip * part, part), :], dq_hbm.at[pl.ds(strip * part, part), :])
        for strip in range(STRIPS)
    ] + [(dk_ref, dk_hbm), (dv_ref, dv_hbm)]
    copies = [
        pltpu.make_async_copy(source, target, sems.at[index])
        for index, (source, target) in enumerate(moves)
    ]
    for copy in copies:
        copy.start()
    for copy in copies:
        copy.wait()


def solution(mesh):
    n_tok = mesh.shape["tok"]
    n_head = mesh.shape["head"]
    slots = REACH + 1
    bf16, f32 = jnp.bfloat16, jnp.float32

    def per_device(query, keys, values, out_grad, log_norm, row_dot, doc_start, spans):
        starts = doc_start.reshape(n_tok, QBLOCK)
        anywhere = pl.BlockSpec(memory_space=pl.ANY)
        outside = pl.BlockSpec(memory_space=pltpu.HBM)
        inside = pl.BlockSpec(memory_space=pltpu.VMEM)
        shapes = (
            jax.ShapeDtypeStruct((QBLOCK, GROUP * HEAD_DIM), bf16),
            jax.ShapeDtypeStruct((QBLOCK, HEAD_DIM), bf16),
            jax.ShapeDtypeStruct((QBLOCK, HEAD_DIM), bf16),
        )
        grads = pl.pallas_call(
            functools.partial(kernel, n_tok, n_head),
            out_shape=tuple(pltpu.VMEM(shape.shape, shape.dtype) for shape in shapes),
            in_specs=[outside] * 8,
            out_specs=(inside,) * 3,
            scratch_shapes=[
                pltpu.VMEM((2, QBLOCK // n_head, KV_HEADS * HEAD_DIM), bf16),
                pltpu.VMEM((2, GROUP * QBLOCK, HEAD_DIM), bf16),
                pltpu.VMEM((2, GROUP, QBLOCK), f32),
                pltpu.VMEM((n_tok, QBLOCK), jnp.int32),
                pltpu.SMEM((n_tok,), jnp.int32),
                pltpu.VMEM((slots, QBLOCK, HEAD_DIM), bf16),
                pltpu.VMEM((slots, QBLOCK, HEAD_DIM), bf16),
                pltpu.VMEM((HEAD_DIM, slots * QBLOCK), bf16),
                pltpu.VMEM((slots, QBLOCK, GROUP * QBLOCK), bf16),
                pltpu.VMEM((QBLOCK, GROUP * QBLOCK), f32),
                pltpu.VMEM((REACH, 2, QBLOCK, HEAD_DIM), bf16),
                pltpu.VMEM((REACH, 2, QBLOCK, HEAD_DIM), bf16),
                pltpu.VMEM((REACH, 2, QBLOCK, HEAD_DIM), bf16),
                pltpu.VMEM((slots, 2, QBLOCK, HEAD_DIM), f32),
                pltpu.SemaphoreType.DMA(()),
                pltpu.SemaphoreType.DMA((4,)),
                pltpu.SemaphoreType.DMA(()),
                pltpu.SemaphoreType.DMA((2,)),
                pltpu.SemaphoreType.DMA((REACH - 1,)),
                pltpu.SemaphoreType.DMA(((REACH - 1) * 2 * PIECES + 2,)),
                pltpu.SemaphoreType.DMA((REACH,)),
                pltpu.SemaphoreType.DMA((REACH,)),
                pltpu.SemaphoreType.DMA((REACH - JOIN,)),
                pltpu.SemaphoreType.DMA(()),
                pltpu.SemaphoreType.REGULAR,
            ],
            compiler_params=pltpu.CompilerParams(
                collective_id=0, has_side_effects=True
            ),
        )(query, keys, values, out_grad, log_norm, row_dot, starts, spans)
        return pl.pallas_call(
            store,
            out_shape=shapes,
            in_specs=[inside] * 3,
            out_specs=(anywhere,) * 3,
            scratch_shapes=[pltpu.SemaphoreType.DMA((STRIPS + 2,))],
            compiler_params=pltpu.CompilerParams(vmem_limit_bytes=4 << 20),
        )(*grads)

    return jax.shard_map(
        per_device,
        mesh=mesh,
        in_specs=(
            P("tok", "head"),
            P(("tok", "head"), None),
            P(("tok", "head"), None),
            P("tok", "head"),
            P("head", "tok"),
            P("head", "tok"),
            P(),
            P(),
        ),
        out_specs=(P("tok", "head"), P("tok", "head"), P("tok", "head")),
        check_vma=False,
    )
```

```python
import functools
import math

import jax
import jax.numpy as jnp
from jax import lax
from jax.experimental import pallas as pl
from jax.experimental.pallas import tpu as pltpu
from jax.sharding import PartitionSpec as P

HEADS = 64
KV_HEADS = 8
HEAD_DIM = 128
QBLOCK = 128
REACH = 5
GROUP = HEADS // KV_HEADS
PIECES = 4
STRIPS = 4
MESH = pl.DeviceIdType.MESH
FAR = 1 << 30
NS = jax.named_scope
JOIN = 4
ROW = 32

NT = (((1,), (1,)), ((), ()))
NN = (((1,), (0,)), ((), ()))


def matmul(a, b, dims):
    return lax.dot_general(a, b, dims, preferred_element_type=jnp.float32)


def kernel(
    n_tok,
    n_head,
    query_hbm,
    keys_hbm,
    values_hbm,
    outgrad_hbm,
    norm_hbm,
    dot_hbm,
    starts_hbm,
    spans_hbm,
    dq_out,
    dk_out,
    dv_out,
    stage_s,
    rows_s,
    norms_s,
    starts_s,
    spans_s,
    key_win,
    value_win,
    key_t,
    ds_all,
    probs_s,
    send_buf,
    recv_buf,
    join_buf,
    terms,
    stage_sem,
    in_sem,
    a2a_send,
    own_sem,
    kv_send,
    kv_recv,
    grad_send,
    grad_recv,
    join_recv,
    next_send,
    turn,
):
    scale = 1.0 / math.sqrt(HEAD_DIM)
    tok = lax.axis_index("tok")
    head = lax.axis_index("head")
    rows = QBLOCK // n_head
    half = QBLOCK // PIECES

    place = lax.rem(tok, ROW)

    def tok_at(step):
        return lax.rem(tok + (step + n_tok), n_tok)

    slot_rows = pl.ds(pl.multiple_of(head * rows, rows), rows)
    my_half = lax.div(head, n_head // PIECES)

    def columns(h):
        return pl.ds(pl.multiple_of(h * HEAD_DIM, HEAD_DIM), HEAD_DIM)

    barrier = pltpu.get_barrier_semaphore()
    with NS("xsig"):
        for step in range(1, n_head):
            pl.semaphore_signal(
                barrier, 1, device_id={"head": lax.rem(head + step, n_head)}, device_id_type=MESH
            )

        @pl.when(tok > 0)
        def _():
            for step in range(n_head):
                pl.semaphore_signal(
                    barrier,
                    1,
                    device_id={"tok": tok_at(-1), "head": lax.rem(head + step, n_head)},
                    device_id_type=MESH,
                )

    sides = ((keys_hbm, stage_s.at[0], key_win), (values_hbm, stage_s.at[1], value_win))
    q_s, do_s = rows_s.at[0], rows_s.at[1]
    norm_s, dot_s = norms_s.at[0], norms_s.at[1]
    with NS("xld"):
        for side, (source, stage, window) in enumerate(sides):
            pltpu.make_async_copy(
                source.at[:, columns(head)], window.at[0, slot_rows, :], own_sem.at[side]
            ).start()
            pltpu.make_async_copy(source, stage, stage_sem).start()
        for h in range(GROUP):
            block = pl.ds(h * QBLOCK, QBLOCK)
            cols = pl.ds(h * HEAD_DIM, HEAD_DIM)
            pltpu.make_async_copy(query_hbm.at[:, cols], q_s.at[block, :], in_sem.at[0]).start()
            pltpu.make_async_copy(outgrad_hbm.at[:, cols], do_s.at[block, :], in_sem.at[0]).start()
        pltpu.make_async_copy(norm_hbm, norm_s, in_sem.at[1]).start()
        pltpu.make_async_copy(dot_hbm, dot_s, in_sem.at[1]).start()
        pltpu.make_async_copy(starts_hbm, starts_s, in_sem.at[2]).start()
        pltpu.make_async_copy(spans_hbm, spans_s, in_sem.at[3]).start()

    def finished(view, sem):
        pltpu.make_async_copy(view, view, sem).wait()

    with NS("xstage"):
        finished(stage_s, stage_sem)
    with NS("xbar"):
        waits = n_head - 1 + jnp.where(tok + 1 < n_tok, n_head, 0)
        pl.semaphore_wait(barrier, waits)

    def to_next(side, step):
        _, stage, window = sides[side]
        peer = lax.rem(head + step, n_head)
        return pltpu.make_async_remote_copy(
            src_ref=stage.at[:, columns(peer)],
            dst_ref=window.at[1, slot_rows, :],
            send_sem=next_send,
            recv_sem=kv_recv.at[side * PIECES + my_half],
            device_id={"tok": tok_at(1), "head": peer},
            device_id_type=MESH,
        )

    order = sorted(range(n_head), key=lambda step: abs(step - n_head // 2))
    order.sort(key=lambda step: step == 0)
    with NS("xspread"):
        for side, (_, stage, window) in enumerate(sides):

            @pl.when(tok + 1 < n_tok)
            def _():
                for step in order:
                    to_next(side, step).start()

        for side, (_, stage, window) in enumerate(sides):
            for step in order[:-1]:
                peer = lax.rem(head + step, n_head)
                pltpu.make_async_remote_copy(
                    src_ref=stage.at[:, columns(peer)],
                    dst_ref=window.at[0, slot_rows, :],
                    send_sem=a2a_send,
                    recv_sem=own_sem.at[side],
                    device_id={"head": peer},
                    device_id_type=MESH,
                ).start()

    def piece(slot, side, part):
        window = (key_win, value_win)[side]
        return window.at[slot, pl.ds(part * half, half), :]

    def arrival(slot, side, part):
        index = (slot - 1) * 2 * PIECES
        return kv_recv.at[index + (side if slot == REACH else side * PIECES + part)]

    def forward(slot, side, part):
        return pltpu.make_async_remote_copy(
            src_ref=piece(slot, side, part),
            dst_ref=piece(slot + 1, side, part),
            send_sem=kv_send.at[slot - 1],
            recv_sem=arrival(slot + 1, side, part),
            device_id={"tok": tok_at(1)},
            device_id_type=MESH,
        )

    def forwards(slot):
        return (tok >= slot) & (tok + 1 < n_tok)

    pieces = [(side, part) for side in range(2) for part in range(PIECES)]
    with NS("xloads"):
        finished(rows_s, in_sem.at[0])
        finished(norms_s, in_sem.at[1])
        finished(starts_s, in_sem.at[2])
        finished(spans_s, in_sem.at[3])

    start_row = starts_s[pl.ds(tok, 1), :]
    span = spans_s[tok]
    row_iota = lax.broadcasted_iota(jnp.int32, (QBLOCK, QBLOCK), 0)
    col_iota = lax.broadcasted_iota(jnp.int32, (QBLOCK, QBLOCK), 1)

    def mask(slot):
        key_pos = row_iota + (tok - slot) * QBLOCK
        allowed = key_pos >= jnp.where(slot < span, start_row, FAR)
        if slot == 0:
            allowed = allowed & (row_iota <= col_iota)
        return allowed

    def pair_probs(key, pair, allowed):
        scores = matmul(key, q_s[pl.ds(pair * 2 * QBLOCK, 2 * QBLOCK), :], NT)
        probs = []
        for e in range(2):
            part = scores[:, e * QBLOCK : (e + 1) * QBLOCK] * scale
            part = jnp.exp(part - norm_s[pl.ds(pair * 2 + e, 1), :])
            probs.append(jnp.where(allowed, part, 0.0))
        return probs

    def pair_grads(value, pair, probs):
        prob_grad = matmul(value, do_s[pl.ds(pair * 2 * QBLOCK, 2 * QBLOCK), :], NT)
        grads = []
        for e in range(2):
            part = prob_grad[:, e * QBLOCK : (e + 1) * QBLOCK]
            part = probs[e] * (part - dot_s[pl.ds(pair * 2 + e, 1), :])
            grads.append(part.astype(jnp.bfloat16))
        return jnp.concatenate(grads, axis=1)

    def lowered(probs):
        return jnp.concatenate([part.astype(jnp.bfloat16) for part in probs], axis=1)

    def block(slot):
        key = key_win[slot]
        value = value_win[slot]
        allowed = mask(slot)
        value_term = jnp.zeros((QBLOCK, HEAD_DIM), jnp.float32)
        key_term = jnp.zeros((QBLOCK, HEAD_DIM), jnp.float32)
        for pair in range(GROUP // 2):
            rows_of = pl.ds(pair * 2 * QBLOCK, 2 * QBLOCK)
            probs = pair_probs(key, pair, allowed)
            grad = pair_grads(value, pair, probs)
            ds_all[slot, :, rows_of] = grad
            value_term = value_term + matmul(lowered(probs), do_s[rows_of, :], NN)
            key_term = key_term + matmul(grad, q_s[rows_of, :], NN)
        key_t[:, pl.ds(slot * QBLOCK, QBLOCK)] = key.T
        return key_term * scale, value_term

    def value_half(slot):
        key = key_win[slot]
        allowed = mask(slot)
        value_term = jnp.zeros((QBLOCK, HEAD_DIM), jnp.float32)
        for pair in range(GROUP // 2):
            rows_of = pl.ds(pair * 2 * QBLOCK, 2 * QBLOCK)
            probs = pair_probs(key, pair, allowed)
            for e in range(2):
                probs_s[:, pl.ds((pair * 2 + e) * QBLOCK, QBLOCK)] = probs[e]
            value_term = value_term + matmul(lowered(probs), do_s[rows_of, :], NN)
        key_t[:, pl.ds(slot * QBLOCK, QBLOCK)] = key.T
        terms[slot, 1] = value_term

    def key_half(slot):
        value = value_win[slot]
        key_term = jnp.zeros((QBLOCK, HEAD_DIM), jnp.float32)
        for pair in range(GROUP // 2):
            rows_of = pl.ds(pair * 2 * QBLOCK, 2 * QBLOCK)
            probs = [probs_s[:, pl.ds((pair * 2 + e) * QBLOCK, QBLOCK)] for e in range(2)]
            grad = pair_grads(value, pair, probs)
            ds_all[slot, :, rows_of] = grad
            key_term = key_term + matmul(grad, q_s[rows_of, :], NN)
        terms[slot, 0] = key_term * scale

    def home(slot):
        return pltpu.make_async_remote_copy(
            src_ref=send_buf.at[slot - 1],
            dst_ref=recv_buf.at[slot - 1],
            send_sem=grad_send.at[slot - 1],
            recv_sem=grad_recv.at[slot - 1],
            device_id={"tok": tok_at(-slot)},
            device_id_type=MESH,
        )

    def onward(slot):
        return pltpu.make_async_remote_copy(
            src_ref=send_buf.at[slot - 1],
            dst_ref=join_buf.at[slot - 1],
            send_sem=grad_send.at[slot - 1],
            recv_sem=join_recv.at[slot - JOIN],
            device_id={"tok": tok_at(1)},
            device_id_type=MESH,
        )

    def goes_on(slot):
        if slot < JOIN or slot == REACH:
            return False
        return place != ROW - 1

    def joins(slot):
        if slot <= JOIN:
            return False
        return (place != 0) & (tok >= slot)

    def compute(slot):
        with NS(f"xblock{slot}"):
            both = block(slot)
            for side in range(2):
                terms[slot, side] = both[side]

    def ship(slot):
        with NS(f"xship{slot}"):
            if joins(slot) is False:
                for side in range(2):
                    send_buf[slot - 1, side] = terms[slot, side].astype(jnp.bfloat16)
            else:

                @pl.when(joins(slot))
                def _():
                    onward(slot - 1).wait_recv()
                    for side in range(2):
                        send_buf[slot - 1, side] = (
                            terms[slot, side] + join_buf[slot - 2, side].astype(jnp.float32)
                        ).astype(jnp.bfloat16)

                @pl.when(jnp.logical_not(joins(slot)))
                def _():
                    for side in range(2):
                        send_buf[slot - 1, side] = terms[slot, side].astype(jnp.bfloat16)

            passing = goes_on(slot)
            if passing is False:
                home(slot).start()
            else:

                @pl.when(passing)
                def _():
                    onward(slot).start()

                @pl.when(jnp.logical_not(passing))
                def _():
                    home(slot).start()

    def home_side(side):
        return pltpu.make_async_remote_copy(
            src_ref=send_buf.at[REACH - 1, side],
            dst_ref=recv_buf.at[REACH - 1, side],
            send_sem=grad_send.at[REACH - 1],
            recv_sem=grad_recv.at[REACH - 1],
            device_id={"tok": tok_at(-REACH)},
            device_id_type=MESH,
        )

    early = (place == 0) & (tok >= REACH)

    crossing = (place < REACH) & (tok >= ROW)

    def pass_turn():
        @pl.when(crossing & (place < REACH - 1))
        def _():
            pl.semaphore_signal(turn, 1, device_id={"tok": tok_at(1)}, device_id_type=MESH)

    def early_side(side):
        @pl.when(early)
        def _():
            send_buf[REACH - 1, side] = terms[REACH, side].astype(jnp.bfloat16)
            home_side(side).start()
            if side == 1:
                pass_turn()

    def arrive(slot):
        for side, part in pieces:
            with NS(f"xkv{slot}{side}{part}"):
                finished(piece(slot, side, part), arrival(slot, side, part))

            @pl.when(forwards(slot))
            def _():
                forward(slot, side, part).start()

    def last():
        with NS("xkv500"):
            finished(key_win.at[REACH], arrival(REACH, 0, 0))
        with NS("xhalf"):
            value_half(REACH)
        early_side(1)
        with NS("xkv510"):
            finished(value_win.at[REACH], arrival(REACH, 1, 0))
        with NS("xblock5"):
            key_half(REACH)
        early_side(0)

    def first():
        with NS("xa2a"):
            for side in range(2):
                finished(sides[side][2].at[0], own_sem.at[side])
        compute(0)

    @pl.when(place == 0)
    def _():
        first()

    for slot in range(1, REACH + 1):

        @pl.when(tok >= slot)
        def _():
            if slot == REACH:
                last()
            else:
                arrive(slot)
                if slot == 1:

                    @pl.when(place != 0)
                    def _():
                        first()

                compute(slot)
                ship(slot)

        @pl.when(tok < slot)
        def _():
            ds_all[slot] = jnp.zeros((QBLOCK, GROUP * QBLOCK), jnp.bfloat16)
            key_t[:, pl.ds(slot * QBLOCK, QBLOCK)] = jnp.zeros((HEAD_DIM, QBLOCK), jnp.bfloat16)

    with NS("xdq"):
        for pair in range(GROUP // 2):
            lanes = pl.ds(pair * 2 * QBLOCK, 2 * QBLOCK)
            grad = ds_all[:, :, lanes].reshape((REACH + 1) * QBLOCK, 2 * QBLOCK)
            dq_t = matmul(key_t[...], grad, NN) * scale
            for e in range(2):
                h = pair * 2 + e
                dq_out[:, pl.ds(h * HEAD_DIM, HEAD_DIM)] = (
                    dq_t[:, e * QBLOCK : (e + 1) * QBLOCK].T.astype(jnp.bfloat16)
                )

    @pl.when((tok >= REACH) & jnp.logical_not(early))
    def _():
        @pl.when(crossing)
        def _():
            pl.semaphore_wait(turn, 1)

        ship(REACH)
        pass_turn()

    for slot in range(1, REACH + 1):
        expected = tok + slot < n_tok
        if JOIN <= slot < REACH:
            expected = place + slot == ROW - 1
        with NS(f"xgrad{slot}"):

            @pl.when(expected)
            def _():
                home(slot).wait_recv()
                for side in range(2):
                    terms[0, side] += recv_buf[slot - 1, side].astype(jnp.float32)

    for side, out in enumerate((dk_out, dv_out)):
        out[...] = terms[0, side].astype(jnp.bfloat16)
    with NS("xsends"):
        finished(q_s.at[pl.ds(0, 2 * (n_head - 1) * rows), :], a2a_send)

        @pl.when(tok + 1 < n_tok)
        def _():
            finished(q_s.at[pl.ds(0, 2 * n_head * rows), :], next_send)

        for slot in range(1, REACH):

            @pl.when(forwards(slot))
            def _():
                finished(q_s.at[pl.ds(0, 2 * QBLOCK), :], kv_send.at[slot - 1])

    with NS("xsendg"):
        for slot in range(1, REACH + 1):

            @pl.when(tok >= slot)
            def _():
                home(slot).wait_send()


def store(dq_ref, dk_ref, dv_ref, dq_hbm, dk_hbm, dv_hbm, sems):
    part = QBLOCK // STRIPS
    moves = [
        (dq_ref.at[pl.ds(strip * part, part), :], dq_hbm.at[pl.ds(strip * part, part), :])
        for strip in range(STRIPS)
    ] + [(dk_ref, dk_hbm), (dv_ref, dv_hbm)]
    copies = [
        pltpu.make_async_copy(source, target, sems.at[index])
        for index, (source, target) in enumerate(moves)
    ]
    for copy in copies:
        copy.start()
    for copy in copies:
        copy.wait()


def solution(mesh):
    n_tok = mesh.shape["tok"]
    n_head = mesh.shape["head"]
    slots = REACH + 1
    bf16, f32 = jnp.bfloat16, jnp.float32

    def per_device(query, keys, values, out_grad, log_norm, row_dot, doc_start, spans):
        starts = doc_start.reshape(n_tok, QBLOCK)
        anywhere = pl.BlockSpec(memory_space=pl.ANY)
        outside = pl.BlockSpec(memory_space=pltpu.HBM)
        inside = pl.BlockSpec(memory_space=pltpu.VMEM)
        shapes = (
            jax.ShapeDtypeStruct((QBLOCK, GROUP * HEAD_DIM), bf16),
            jax.ShapeDtypeStruct((QBLOCK, HEAD_DIM), bf16),
            jax.ShapeDtypeStruct((QBLOCK, HEAD_DIM), bf16),
        )
        grads = pl.pallas_call(
            functools.partial(kernel, n_tok, n_head),
            out_shape=tuple(pltpu.VMEM(shape.shape, shape.dtype) for shape in shapes),
            in_specs=[outside] * 8,
            out_specs=(inside,) * 3,
            scratch_shapes=[
                pltpu.VMEM((2, QBLOCK // n_head, KV_HEADS * HEAD_DIM), bf16),
                pltpu.VMEM((2, GROUP * QBLOCK, HEAD_DIM), bf16),
                pltpu.VMEM((2, GROUP, QBLOCK), f32),
                pltpu.VMEM((n_tok, QBLOCK), jnp.int32),
                pltpu.SMEM((n_tok,), jnp.int32),
                pltpu.VMEM((slots, QBLOCK, HEAD_DIM), bf16),
                pltpu.VMEM((slots, QBLOCK, HEAD_DIM), bf16),
                pltpu.VMEM((HEAD_DIM, slots * QBLOCK), bf16),
                pltpu.VMEM((slots, QBLOCK, GROUP * QBLOCK), bf16),
                pltpu.VMEM((QBLOCK, GROUP * QBLOCK), f32),
                pltpu.VMEM((REACH, 2, QBLOCK, HEAD_DIM), bf16),
                pltpu.VMEM((REACH, 2, QBLOCK, HEAD_DIM), bf16),
                pltpu.VMEM((REACH, 2, QBLOCK, HEAD_DIM), bf16),
                pltpu.VMEM((slots, 2, QBLOCK, HEAD_DIM), f32),
                pltpu.SemaphoreType.DMA(()),
                pltpu.SemaphoreType.DMA((4,)),
                pltpu.SemaphoreType.DMA(()),
                pltpu.SemaphoreType.DMA((2,)),
                pltpu.SemaphoreType.DMA((REACH - 1,)),
                pltpu.SemaphoreType.DMA(((REACH - 1) * 2 * PIECES + 2,)),
                pltpu.SemaphoreType.DMA((REACH,)),
                pltpu.SemaphoreType.DMA((REACH,)),
                pltpu.SemaphoreType.DMA((REACH - JOIN,)),
                pltpu.SemaphoreType.DMA(()),
                pltpu.SemaphoreType.REGULAR,
            ],
            compiler_params=pltpu.CompilerParams(
                collective_id=0, has_side_effects=True
            ),
        )(query, keys, values, out_grad, log_norm, row_dot, starts, spans)
        return pl.pallas_call(
            store,
            out_shape=shapes,
            in_specs=[inside] * 3,
            out_specs=(anywhere,) * 3,
            scratch_shapes=[pltpu.SemaphoreType.DMA((STRIPS + 2,))],
            compiler_params=pltpu.CompilerParams(vmem_limit_bytes=4 << 20),
        )(*grads)

    return jax.shard_map(
        per_device,
        mesh=mesh,
        in_specs=(
            P("tok", "head"),
            P(("tok", "head"), None),
            P(("tok", "head"), None),
            P("tok", "head"),
            P("head", "tok"),
            P("head", "tok"),
            P(),
            P(),
        ),
        out_specs=(P("tok", "head"), P("tok", "head"), P("tok", "head")),
        check_vma=False,
    )
```

```python
import functools
import math

import jax
import jax.numpy as jnp
from jax import lax
from jax.experimental import pallas as pl
from jax.experimental.pallas import tpu as pltpu
from jax.sharding import PartitionSpec as P

HEADS = 64
KV_HEADS = 8
HEAD_DIM = 128
QBLOCK = 128
REACH = 5
GROUP = HEADS // KV_HEADS
PIECES = 4
STRIPS = 4
MESH = pl.DeviceIdType.MESH
FAR = 1 << 30
NS = jax.named_scope
JOIN = 4
ROW = 32

NT = (((1,), (1,)), ((), ()))
NN = (((1,), (0,)), ((), ()))


def matmul(a, b, dims):
    return lax.dot_general(a, b, dims, preferred_element_type=jnp.float32)


def kernel(
    n_tok,
    n_head,
    query_hbm,
    keys_hbm,
    values_hbm,
    outgrad_hbm,
    norm_hbm,
    dot_hbm,
    starts_hbm,
    spans_hbm,
    dq_out,
    dk_out,
    dv_out,
    stage_s,
    rows_s,
    norms_s,
    starts_s,
    spans_s,
    key_win,
    value_win,
    key_t,
    ds_all,
    probs_s,
    send_buf,
    recv_buf,
    join_buf,
    terms,
    stage_sem,
    in_sem,
    a2a_send,
    own_sem,
    kv_send,
    kv_recv,
    grad_send,
    grad_recv,
    join_recv,
    next_send,
    turn,
):
    scale = 1.0 / math.sqrt(HEAD_DIM)
    tok = lax.axis_index("tok")
    head = lax.axis_index("head")
    rows = QBLOCK // n_head
    half = QBLOCK // PIECES

    place = lax.rem(tok, ROW)

    def tok_at(step):
        return lax.rem(tok + (step + n_tok), n_tok)

    slot_rows = pl.ds(pl.multiple_of(head * rows, rows), rows)
    my_half = lax.div(head, n_head // PIECES)

    def columns(h):
        return pl.ds(pl.multiple_of(h * HEAD_DIM, HEAD_DIM), HEAD_DIM)

    barrier = pltpu.get_barrier_semaphore()
    with NS("xsig"):
        for step in range(1, n_head):
            pl.semaphore_signal(
                barrier, 1, device_id={"head": lax.rem(head + step, n_head)}, device_id_type=MESH
            )

        @pl.when(tok > 0)
        def _():
            for step in range(n_head):
                pl.semaphore_signal(
                    barrier,
                    1,
                    device_id={"tok": tok_at(-1), "head": lax.rem(head + step, n_head)},
                    device_id_type=MESH,
                )

    sides = ((keys_hbm, stage_s.at[0], key_win), (values_hbm, stage_s.at[1], value_win))
    q_s, do_s = rows_s.at[0], rows_s.at[1]
    norm_s, dot_s = norms_s.at[0], norms_s.at[1]
    with NS("xld"):
        for side, (source, stage, window) in enumerate(sides):
            pltpu.make_async_copy(
                source.at[:, columns(head)], window.at[0, slot_rows, :], own_sem.at[side]
            ).start()
            pltpu.make_async_copy(source, stage, stage_sem).start()
        for h in range(GROUP):
            block = pl.ds(h * QBLOCK, QBLOCK)
            cols = pl.ds(h * HEAD_DIM, HEAD_DIM)
            pltpu.make_async_copy(query_hbm.at[:, cols], q_s.at[block, :], in_sem.at[0]).start()
            pltpu.make_async_copy(outgrad_hbm.at[:, cols], do_s.at[block, :], in_sem.at[0]).start()
        pltpu.make_async_copy(norm_hbm, norm_s, in_sem.at[1]).start()
        pltpu.make_async_copy(dot_hbm, dot_s, in_sem.at[1]).start()
        pltpu.make_async_copy(starts_hbm, starts_s, in_sem.at[2]).start()
        pltpu.make_async_copy(spans_hbm, spans_s, in_sem.at[3]).start()

    def finished(view, sem):
        pltpu.make_async_copy(view, view, sem).wait()

    with NS("xstage"):
        finished(stage_s, stage_sem)
    with NS("xbar"):
        waits = n_head - 1 + jnp.where(tok + 1 < n_tok, n_head, 0)
        pl.semaphore_wait(barrier, waits)

    def to_next(side, step):
        _, stage, window = sides[side]
        peer = lax.rem(head + step, n_head)
        return pltpu.make_async_remote_copy(
            src_ref=stage.at[:, columns(peer)],
            dst_ref=window.at[1, slot_rows, :],
            send_sem=next_send,
            recv_sem=kv_recv.at[side * PIECES + my_half],
            device_id={"tok": tok_at(1), "head": peer},
            device_id_type=MESH,
        )

    order = sorted(range(n_head), key=lambda step: abs(step - n_head // 2))
    order.sort(key=lambda step: step == 0)
    with NS("xspread"):
        for side, (_, stage, window) in enumerate(sides):

            @pl.when(tok + 1 < n_tok)
            def _():
                for step in order:
                    to_next(side, step).start()

        for side, (_, stage, window) in enumerate(sides):
            for step in order[:-1]:
                peer = lax.rem(head + step, n_head)
                pltpu.make_async_remote_copy(
                    src_ref=stage.at[:, columns(peer)],
                    dst_ref=window.at[0, slot_rows, :],
                    send_sem=a2a_send,
                    recv_sem=own_sem.at[side],
                    device_id={"head": peer},
                    device_id_type=MESH,
                ).start()

    def piece(slot, side, part):
        window = (key_win, value_win)[side]
        return window.at[slot, pl.ds(part * half, half), :]

    def arrival(slot, side, part):
        index = (slot - 1) * 2 * PIECES
        return kv_recv.at[index + (side if slot == REACH else side * PIECES + part)]

    def forward(slot, side, part):
        return pltpu.make_async_remote_copy(
            src_ref=piece(slot, side, part),
            dst_ref=piece(slot + 1, side, part),
            send_sem=kv_send.at[slot - 1],
            recv_sem=arrival(slot + 1, side, part),
            device_id={"tok": tok_at(1)},
            device_id_type=MESH,
        )

    def forwards(slot):
        return (tok >= slot) & (tok + 1 < n_tok)

    pieces = [(side, part) for side in range(2) for part in range(PIECES)]
    with NS("xloads"):
        finished(rows_s, in_sem.at[0])
        finished(norms_s, in_sem.at[1])
        finished(starts_s, in_sem.at[2])
        finished(spans_s, in_sem.at[3])

    start_row = starts_s[pl.ds(tok, 1), :]
    span = spans_s[tok]
    row_iota = lax.broadcasted_iota(jnp.int32, (QBLOCK, QBLOCK), 0)
    col_iota = lax.broadcasted_iota(jnp.int32, (QBLOCK, QBLOCK), 1)

    def mask(slot):
        key_pos = row_iota + (tok - slot) * QBLOCK
        allowed = key_pos >= jnp.where(slot < span, start_row, FAR)
        if slot == 0:
            allowed = allowed & (row_iota <= col_iota)
        return allowed

    def pair_probs(key, pair, allowed):
        scores = matmul(key, q_s[pl.ds(pair * 2 * QBLOCK, 2 * QBLOCK), :], NT)
        probs = []
        for e in range(2):
            part = scores[:, e * QBLOCK : (e + 1) * QBLOCK] * scale
            part = jnp.exp(part - norm_s[pl.ds(pair * 2 + e, 1), :])
            probs.append(jnp.where(allowed, part, 0.0))
        return probs

    def pair_grads(value, pair, probs):
        prob_grad = matmul(value, do_s[pl.ds(pair * 2 * QBLOCK, 2 * QBLOCK), :], NT)
        grads = []
        for e in range(2):
            part = prob_grad[:, e * QBLOCK : (e + 1) * QBLOCK]
            part = probs[e] * (part - dot_s[pl.ds(pair * 2 + e, 1), :])
            grads.append(part.astype(jnp.bfloat16))
        return jnp.concatenate(grads, axis=1)

    def lowered(probs):
        return jnp.concatenate([part.astype(jnp.bfloat16) for part in probs], axis=1)

    def block(slot):
        key = key_win[slot]
        value = value_win[slot]
        allowed = mask(slot)
        value_term = jnp.zeros((QBLOCK, HEAD_DIM), jnp.float32)
        key_term = jnp.zeros((QBLOCK, HEAD_DIM), jnp.float32)
        for pair in range(GROUP // 2):
            rows_of = pl.ds(pair * 2 * QBLOCK, 2 * QBLOCK)
            probs = pair_probs(key, pair, allowed)
            grad = pair_grads(value, pair, probs)
            ds_all[slot, :, rows_of] = grad
            value_term = value_term + matmul(lowered(probs), do_s[rows_of, :], NN)
            key_term = key_term + matmul(grad, q_s[rows_of, :], NN)
        key_t[:, pl.ds(slot * QBLOCK, QBLOCK)] = key.T
        return key_term * scale, value_term

    def value_half(slot):
        key = key_win[slot]
        allowed = mask(slot)
        value_term = jnp.zeros((QBLOCK, HEAD_DIM), jnp.float32)
        for pair in range(GROUP // 2):
            rows_of = pl.ds(pair * 2 * QBLOCK, 2 * QBLOCK)
            probs = pair_probs(key, pair, allowed)
            for e in range(2):
                probs_s[:, pl.ds((pair * 2 + e) * QBLOCK, QBLOCK)] = probs[e]
            value_term = value_term + matmul(lowered(probs), do_s[rows_of, :], NN)
        key_t[:, pl.ds(slot * QBLOCK, QBLOCK)] = key.T
        terms[slot, 1] = value_term

    def key_half(slot):
        value = value_win[slot]
        key_term = jnp.zeros((QBLOCK, HEAD_DIM), jnp.float32)
        for pair in range(GROUP // 2):
            rows_of = pl.ds(pair * 2 * QBLOCK, 2 * QBLOCK)
            probs = [probs_s[:, pl.ds((pair * 2 + e) * QBLOCK, QBLOCK)] for e in range(2)]
            grad = pair_grads(value, pair, probs)
            ds_all[slot, :, rows_of] = grad
            key_term = key_term + matmul(grad, q_s[rows_of, :], NN)
        terms[slot, 0] = key_term * scale

    def home(slot):
        return pltpu.make_async_remote_copy(
            src_ref=send_buf.at[slot - 1],
            dst_ref=recv_buf.at[slot - 1],
            send_sem=grad_send.at[slot - 1],
            recv_sem=grad_recv.at[slot - 1],
            device_id={"tok": tok_at(-slot)},
            device_id_type=MESH,
        )

    def onward(slot):
        return pltpu.make_async_remote_copy(
            src_ref=send_buf.at[slot - 1],
            dst_ref=join_buf.at[slot - 1],
            send_sem=grad_send.at[slot - 1],
            recv_sem=join_recv.at[slot - JOIN],
            device_id={"tok": tok_at(1)},
            device_id_type=MESH,
        )

    def goes_on(slot):
        if slot < JOIN or slot == REACH:
            return False
        return place != ROW - 1

    def joins(slot):
        if slot <= JOIN:
            return False
        return (place != 0) & (tok >= slot)

    def compute(slot):
        with NS(f"xblock{slot}"):
            both = block(slot)
            for side in range(2):
                terms[slot, side] = both[side]

    def ship(slot):
        with NS(f"xship{slot}"):
            if joins(slot) is False:
                for side in range(2):
                    send_buf[slot - 1, side] = terms[slot, side].astype(jnp.bfloat16)
            else:

                @pl.when(joins(slot))
                def _():
                    onward(slot - 1).wait_recv()
                    for side in range(2):
                        send_buf[slot - 1, side] = (
                            terms[slot, side] + join_buf[slot - 2, side].astype(jnp.float32)
                        ).astype(jnp.bfloat16)

                @pl.when(jnp.logical_not(joins(slot)))
                def _():
                    for side in range(2):
                        send_buf[slot - 1, side] = terms[slot, side].astype(jnp.bfloat16)

            passing = goes_on(slot)
            if passing is False:
                home(slot).start()
            else:

                @pl.when(passing)
                def _():
                    onward(slot).start()

                @pl.when(jnp.logical_not(passing))
                def _():
                    home(slot).start()

    def home_side(side):
        return pltpu.make_async_remote_copy(
            src_ref=send_buf.at[REACH - 1, side],
            dst_ref=recv_buf.at[REACH - 1, side],
            send_sem=grad_send.at[REACH - 1],
            recv_sem=grad_recv.at[REACH - 1],
            device_id={"tok": tok_at(-REACH)},
            device_id_type=MESH,
        )

    early = (place == 0) & (tok >= REACH)

    crossing = (place < REACH) & (tok >= ROW)

    def pass_turn():
        @pl.when(crossing & (place < REACH - 1))
        def _():
            pl.semaphore_signal(turn, 1, device_id={"tok": tok_at(1)}, device_id_type=MESH)

    def early_side(side):
        @pl.when(early)
        def _():
            send_buf[REACH - 1, side] = terms[REACH, side].astype(jnp.bfloat16)
            home_side(side).start()
            if side == 1:
                pass_turn()

    def arrive(slot):
        for side, part in pieces:
            with NS(f"xkv{slot}{side}{part}"):
                finished(piece(slot, side, part), arrival(slot, side, part))

            @pl.when(forwards(slot))
            def _():
                forward(slot, side, part).start()

    def last():
        with NS("xkv500"):
            finished(key_win.at[REACH], arrival(REACH, 0, 0))
        with NS("xhalf"):
            value_half(REACH)
        early_side(1)
        with NS("xkv510"):
            finished(value_win.at[REACH], arrival(REACH, 1, 0))
        with NS("xblock5"):
            key_half(REACH)
        early_side(0)

    def first():
        with NS("xa2a"):
            for side in range(2):
                finished(sides[side][2].at[0], own_sem.at[side])
        compute(0)

    @pl.when(place == 0)
    def _():
        first()

    for slot in range(1, REACH + 1):

        @pl.when(tok >= slot)
        def _():
            if slot == REACH:
                last()
            else:
                arrive(slot)
                if slot == 1:

                    @pl.when(place != 0)
                    def _():
                        first()

                compute(slot)
                ship(slot)

        @pl.when(tok < slot)
        def _():
            ds_all[slot] = jnp.zeros((QBLOCK, GROUP * QBLOCK), jnp.bfloat16)
            key_t[:, pl.ds(slot * QBLOCK, QBLOCK)] = jnp.zeros((HEAD_DIM, QBLOCK), jnp.bfloat16)

    with NS("xdq"):
        for pair in range(GROUP // 2):
            lanes = pl.ds(pair * 2 * QBLOCK, 2 * QBLOCK)
            grad = ds_all[:, :, lanes].reshape((REACH + 1) * QBLOCK, 2 * QBLOCK)
            dq_t = matmul(key_t[...], grad, NN) * scale
            for e in range(2):
                h = pair * 2 + e
                dq_out[:, pl.ds(h * HEAD_DIM, HEAD_DIM)] = (
                    dq_t[:, e * QBLOCK : (e + 1) * QBLOCK].T.astype(jnp.bfloat16)
                )

    @pl.when((tok >= REACH) & jnp.logical_not(early))
    def _():
        @pl.when(crossing)
        def _():
            pl.semaphore_wait(turn, 1)

        pass_turn()
        ship(REACH)

    for slot in range(1, REACH + 1):
        expected = tok + slot < n_tok
        if JOIN <= slot < REACH:
            expected = place + slot == ROW - 1
        with NS(f"xgrad{slot}"):

            @pl.when(expected)
            def _():
                home(slot).wait_recv()
                for side in range(2):
                    terms[0, side] += recv_buf[slot - 1, side].astype(jnp.float32)

    for side, out in enumerate((dk_out, dv_out)):
        out[...] = terms[0, side].astype(jnp.bfloat16)
    with NS("xsends"):
        finished(q_s.at[pl.ds(0, 2 * (n_head - 1) * rows), :], a2a_send)

        @pl.when(tok + 1 < n_tok)
        def _():
            finished(q_s.at[pl.ds(0, 2 * n_head * rows), :], next_send)

        for slot in range(1, REACH):

            @pl.when(forwards(slot))
            def _():
                finished(q_s.at[pl.ds(0, 2 * QBLOCK), :], kv_send.at[slot - 1])

    with NS("xsendg"):
        for slot in range(1, REACH + 1):

            @pl.when(tok >= slot)
            def _():
                home(slot).wait_send()


def store(dq_ref, dk_ref, dv_ref, dq_hbm, dk_hbm, dv_hbm, sems):
    part = QBLOCK // STRIPS
    moves = [
        (dq_ref.at[pl.ds(strip * part, part), :], dq_hbm.at[pl.ds(strip * part, part), :])
        for strip in range(STRIPS)
    ] + [(dk_ref, dk_hbm), (dv_ref, dv_hbm)]
    copies = [
        pltpu.make_async_copy(source, target, sems.at[index])
        for index, (source, target) in enumerate(moves)
    ]
    for copy in copies:
        copy.start()
    for copy in copies:
        copy.wait()


def solution(mesh):
    n_tok = mesh.shape["tok"]
    n_head = mesh.shape["head"]
    slots = REACH + 1
    bf16, f32 = jnp.bfloat16, jnp.float32

    def per_device(query, keys, values, out_grad, log_norm, row_dot, doc_start, spans):
        starts = doc_start.reshape(n_tok, QBLOCK)
        anywhere = pl.BlockSpec(memory_space=pl.ANY)
        outside = pl.BlockSpec(memory_space=pltpu.HBM)
        inside = pl.BlockSpec(memory_space=pltpu.VMEM)
        shapes = (
            jax.ShapeDtypeStruct((QBLOCK, GROUP * HEAD_DIM), bf16),
            jax.ShapeDtypeStruct((QBLOCK, HEAD_DIM), bf16),
            jax.ShapeDtypeStruct((QBLOCK, HEAD_DIM), bf16),
        )
        grads = pl.pallas_call(
            functools.partial(kernel, n_tok, n_head),
            out_shape=tuple(pltpu.VMEM(shape.shape, shape.dtype) for shape in shapes),
            in_specs=[outside] * 8,
            out_specs=(inside,) * 3,
            scratch_shapes=[
                pltpu.VMEM((2, QBLOCK // n_head, KV_HEADS * HEAD_DIM), bf16),
                pltpu.VMEM((2, GROUP * QBLOCK, HEAD_DIM), bf16),
                pltpu.VMEM((2, GROUP, QBLOCK), f32),
                pltpu.VMEM((n_tok, QBLOCK), jnp.int32),
                pltpu.SMEM((n_tok,), jnp.int32),
                pltpu.VMEM((slots, QBLOCK, HEAD_DIM), bf16),
                pltpu.VMEM((slots, QBLOCK, HEAD_DIM), bf16),
                pltpu.VMEM((HEAD_DIM, slots * QBLOCK), bf16),
                pltpu.VMEM((slots, QBLOCK, GROUP * QBLOCK), bf16),
                pltpu.VMEM((QBLOCK, GROUP * QBLOCK), f32),
                pltpu.VMEM((REACH, 2, QBLOCK, HEAD_DIM), bf16),
                pltpu.VMEM((REACH, 2, QBLOCK, HEAD_DIM), bf16),
                pltpu.VMEM((REACH, 2, QBLOCK, HEAD_DIM), bf16),
                pltpu.VMEM((slots, 2, QBLOCK, HEAD_DIM), f32),
                pltpu.SemaphoreType.DMA(()),
                pltpu.SemaphoreType.DMA((4,)),
                pltpu.SemaphoreType.DMA(()),
                pltpu.SemaphoreType.DMA((2,)),
                pltpu.SemaphoreType.DMA((REACH - 1,)),
                pltpu.SemaphoreType.DMA(((REACH - 1) * 2 * PIECES + 2,)),
                pltpu.SemaphoreType.DMA((REACH,)),
                pltpu.SemaphoreType.DMA((REACH,)),
                pltpu.SemaphoreType.DMA((REACH - JOIN,)),
                pltpu.SemaphoreType.DMA(()),
                pltpu.SemaphoreType.REGULAR,
            ],
            compiler_params=pltpu.CompilerParams(
                collective_id=0, has_side_effects=True
            ),
        )(query, keys, values, out_grad, log_norm, row_dot, starts, spans)
        return pl.pallas_call(
            store,
            out_shape=shapes,
            in_specs=[inside] * 3,
            out_specs=(anywhere,) * 3,
            scratch_shapes=[pltpu.SemaphoreType.DMA((STRIPS + 2,))],
            compiler_params=pltpu.CompilerParams(vmem_limit_bytes=4 << 20),
        )(*grads)

    return jax.shard_map(
        per_device,
        mesh=mesh,
        in_specs=(
            P("tok", "head"),
            P(("tok", "head"), None),
            P(("tok", "head"), None),
            P("tok", "head"),
            P("head", "tok"),
            P("head", "tok"),
            P(),
            P(),
        ),
        out_specs=(P("tok", "head"), P("tok", "head"), P("tok", "head")),
        check_vma=False,
    )
```
